32 devices in a mesh: groups: 2 (over x), row: 16 (over z, y, core).
Axes of the slice: x: 2, y: 2, z: 4, core: 2. Of those that a mesh axis runs over, the one named last changes fastest.
Arguments:
- object_field: float32 [2, 16384, 384], P(None, ('groups', 'row')), parts along dimension 1, may hold values from -26 to 26
- probe: float32 [2, 2, 256, 256], replicated, may hold values from -4.2 to 4.2
- amplitude: float32 [256, 256, 256], P(('groups', 'row')), parts along dimension 0, may hold values from 0.2 to 27, as said below
- offsets: int32 [256, 2], P(('groups', 'row')), parts along dimension 0, may hold values from 0 to 8191, as said below
Outputs:
- object_grad: float32 [2, 16384, 384], P(None, ('groups', 'row')), parts along dimension 1
- probe_dir: float32 [4, 2, 256, 256], P('groups'), parts along dimension 0
- loss: float32 [2], P('groups'), parts along dimension 0
The draws below stay inside these ranges and needn't reach their ends.
There are 2 independent parts, one for each index of `groups`. The reference program is written for one: setup_inputs(seed, part) draws one part's arguments, and reference() takes and returns one part's arrays. A program takes and returns all parts, laid end to end along the dimension named above; an argument that names none is the same for every part. Nothing has to cross between parts.
Inputs may be any that keep to these rules, and one draw needn't show every extreme that they name: offsets[p, 0] is k * 64 plus a shift below 64 in the rows of device p // 8, with k = p % 8; offsets[p, 1] lies from 0 to 127. `amplitude`: measured amplitudes are positive.
All inputs are finite; a program needn't handle non-finite values.
Results may differ from the reference program's by a relative error of at most 0.0062.
Values sent between devices are 32-bit elements; how exact they have to be, the bound alone decides.
No kernel may reach another device: no remote copies, remote signals or barrier semaphores. Data moves between devices by JAX's collectives and lax.ppermute only.
A program may use at most 128 MiB of HBM per device.

```python
import math
import jax
import jax.numpy as jnp
from jax import lax

PATCH = 256
MODES = 2
STEP = 64
TILE = 512
SPAN = 128
OWIDTH = 384
POS_DEV = 8
POSITIONS = 128
NROWS = 8192
N_ROW = 16


def draw_offsets(key, part):
    first_key, second_key = jax.random.split(jax.random.fold_in(key, 11))
    index = jnp.arange(POSITIONS, dtype=jnp.int32)
    device = index // POS_DEV
    within = index % POS_DEV
    row_shift = jax.random.randint(first_key, (POSITIONS,), 0, STEP, dtype=jnp.int32)
    col_start = jax.random.randint(second_key, (POSITIONS,), 0, SPAN, dtype=jnp.int32)
    first = index == 0
    last = index == POSITIONS - 1
    row_shift = jnp.where(first, 0, jnp.where(last, STEP - 1, row_shift))
    col_start = jnp.where(first, 0, jnp.where(last, SPAN - 1, col_start))
    rows = device * TILE + within * STEP + row_shift
    return jnp.stack([rows, col_start], 1).astype(jnp.int32)


def draw_object_field(key, part):
    base_key, row_key, col_key = jax.random.split(jax.random.fold_in(key, 23), 3)
    row_scale = jnp.exp(jax.random.uniform(row_key, (NROWS,), jnp.float32, math.log(0.3), math.log(3.0)))
    col_scale = jnp.exp(jax.random.uniform(col_key, (OWIDTH,), jnp.float32, math.log(0.3), math.log(3.0)))
    scales = row_scale[:, None] * col_scale[None, :]
    base = jnp.clip(jax.random.normal(base_key, (2, NROWS, OWIDTH), jnp.float32), -4.0, 4.0) * 0.7
    return (base * scales[None]).astype(jnp.float32)


def draw_amplitude(key, part):
    base_key = jax.random.fold_in(key, 37)
    where = jnp.arange(POSITIONS, dtype=jnp.int32).astype(jnp.float32) / max(POSITIONS - 1, 1)
    base = jnp.exp(jax.random.uniform(base_key, (POSITIONS, PATCH, PATCH), jnp.float32, math.log(0.3), math.log(3.0)))
    rise = 1.0 + 2.0 * where
    return (base * rise[:, None, None]).astype(jnp.float32)


def normal_values(own_key, dims, width, bound, kind=jnp.bfloat16):
    drawn = width * jax.random.normal(own_key, dims, jnp.float32)
    return jnp.clip(drawn, min=-bound, max=bound).astype(kind)


def setup_inputs(seed: int = 0, part: int = 0) -> dict:
    key_list = jax.random.split(jax.random.key(seed), 5)
    part_splits = jax.random.split(jax.random.fold_in(key_list[4], part), 5)
    return {
        "object_field": draw_object_field(jax.random.fold_in(jax.random.fold_in(key_list[4], part), 71), part),
        "probe": normal_values(key_list[1], (MODES, 2, PATCH, PATCH), 0.7, 4.2, jnp.float32),
        "amplitude": draw_amplitude(jax.random.fold_in(jax.random.fold_in(key_list[4], part), 71), part),
        "offsets": draw_offsets(jax.random.fold_in(jax.random.fold_in(key_list[4], part), 71), part),
    }


def dft_tables(size):
    idx = jnp.arange(size, dtype=jnp.int32)
    prod = idx[:, None] * idx[None, :] % size
    angle = prod.astype(jnp.float32) * (2.0 * math.pi / size)
    scale = 1.0 / math.sqrt(size)
    cosine = jnp.cos(angle) * scale
    sine = jnp.sin(angle) * scale
    column = jnp.stack([jnp.stack([cosine, -sine], 1), jnp.stack([sine, cosine], 1)], 0).astype(jnp.bfloat16)
    rowwise = jnp.stack([jnp.stack([cosine, sine], 1), jnp.stack([-sine, cosine], 1)], 0).astype(jnp.bfloat16)
    return (column, rowwise)

def mix(form, left, right):
    return jnp.einsum(form, left.astype(jnp.float32), right.astype(jnp.float32), precision=lax.Precision.HIGHEST)

def window_terms(windows, probe, amplitude, column, rowwise):
    o_re = windows[:, 0][:, None]
    o_im = windows[:, 1][:, None]
    p_re = probe[:, 0][None]
    p_im = probe[:, 1][None]
    wave = jnp.stack([p_re * o_re - p_im * o_im, p_re * o_im + p_im * o_re], 2).astype(jnp.bfloat16)
    half = mix('pmcij,cjdk->pmdik', wave, column).astype(jnp.bfloat16)
    far = mix('erdi,pmdil->pmerl', rowwise, half)
    magnitude = jnp.sqrt(lax.optimization_barrier(jnp.sum(far * far, axis=(1, 2))))
    loss_part = jnp.sum((magnitude - amplitude) ** 2)
    weight = 0.25 * (1.0 - amplitude / jnp.maximum(magnitude, 0.5))
    grad_far = (weight[:, None, None] * far).astype(jnp.bfloat16)
    grad_half = mix('erdi,pmerl->pmdil', rowwise, grad_far).astype(jnp.bfloat16)
    grad_wave = mix('pmdik,cjdk->pmcij', grad_half, column)
    g_re = grad_wave[:, :, 0]
    g_im = grad_wave[:, :, 1]
    win_grad = jnp.stack([lax.optimization_barrier(jnp.sum(p_re * g_re + p_im * g_im, 1)), lax.optimization_barrier(jnp.sum(p_re * g_im - p_im * g_re, 1))], 1)
    probe_grad = jnp.stack([lax.optimization_barrier(jnp.sum(o_re * g_re + o_im * g_im, 0)), lax.optimization_barrier(jnp.sum(o_re * g_im - o_im * g_re, 0))], 1)
    illumination = lax.optimization_barrier(jnp.sum(windows[:, 0] ** 2 + windows[:, 1] ** 2, 0))
    return (win_grad, probe_grad, illumination, loss_part)

def reference(object_field, probe, amplitude, offsets):
    column, rowwise = dft_tables(PATCH)
    extended = jnp.concatenate([object_field, jnp.zeros((2, TILE, OWIDTH), jnp.float32)], 1)
    block_offsets = offsets.reshape(N_ROW, POS_DEV, 2)
    block_amps = amplitude.reshape(N_ROW, POS_DEV, PATCH, PATCH)

    def cut(row_start, col_start):
        return lax.dynamic_slice(extended, (jnp.int32(0), row_start.astype(jnp.int32), col_start.astype(jnp.int32)), (2, PATCH, PATCH))

    def visit(carry, block):
        grad_ext, probe_sum, illum_sum, loss_sum = carry
        block_off, block_amp = block
        windows = jax.vmap(cut)(block_off[:, 0], block_off[:, 1])
        win_grad, probe_grad, illumination, loss_part = window_terms(windows, probe, block_amp, column, rowwise)

        def add_one(k, grads):
            start = (jnp.int32(0), block_off[k, 0].astype(jnp.int32), block_off[k, 1].astype(jnp.int32))
            current = lax.dynamic_slice(grads, start, (2, PATCH, PATCH))
            return lax.dynamic_update_slice(grads, current + win_grad[k], start)
        grad_ext = lax.fori_loop(0, POS_DEV, add_one, grad_ext)
        return ((grad_ext, probe_sum + probe_grad, illum_sum + illumination, loss_sum + loss_part), None)
    init = (jnp.zeros((2, NROWS + TILE, OWIDTH), jnp.float32), jnp.zeros((MODES, 2, PATCH, PATCH), jnp.float32), jnp.zeros((PATCH, PATCH), jnp.float32), jnp.zeros((), jnp.float32))
    final, unused = lax.scan(visit, init, (block_offsets, block_amps))
    grad_ext, probe_sum, illum_sum, loss_sum = final
    object_grad = grad_ext[:, :NROWS]
    probe_dir = probe_sum / jnp.sqrt(illum_sum + 1.0)[None, None]
    loss = (loss_sum / (POSITIONS * PATCH * PATCH)).reshape(1)
    return (object_grad, probe_dir, loss)
```

```python
import functools
import math

import jax
import jax.numpy as jnp
import ml_dtypes
import numpy as np
from jax import lax
from jax.experimental import pallas as pl
from jax.experimental.pallas import tpu as pltpu
from jax.sharding import PartitionSpec as P

F32, BF16 = jnp.float32, jnp.bfloat16


def dft_tables(size):
    idx = np.arange(size)
    angle = (idx[:, None] * idx[None, :] % size).astype(np.float32) * np.float32(2.0 * math.pi / size)
    scale = np.float32(1.0 / math.sqrt(size))
    return np.stack([np.cos(angle) * scale, np.sin(angle) * scale]).astype(ml_dtypes.bfloat16)


def windows_kernel(first, off_ref, *refs):
    if first:
        top_ref, bottom_ref, probe_ref, amp_ref, table_ref = refs[:5]
        refs = refs[5:]
        grad_ref, pg_ref, loss_ref = refs[:3]
    else:
        top_ref, bottom_ref, probe_ref, amp_ref, table_ref, pg_in, loss_in = refs[:7]
        refs = refs[7:]
        grad_ref, payload_ref = refs[:2]
    ext, win, wave, mid, far, fwd, adj = refs[-7:]
    if not first:
        pg_ref, loss_ref = refs[2:4]
    k = pl.program_id(0)
    n = probe_ref.shape[-1]
    half_rows = top_ref.shape[1]
    width = ext.shape[2]

    @pl.when(k == 0)
    def _():
        grad_ref[...] = jnp.zeros_like(grad_ref)
        if first:
            pg_ref[...] = jnp.zeros_like(pg_ref)
            loss_ref[...] = jnp.zeros_like(loss_ref)
        else:
            pg_ref[...] = pg_in[...]
            loss_ref[...] = loss_in[...]
        ext[:, :half_rows] = top_ref[...]
        ext[:, half_rows:] = bottom_ref[...]
        cosine, sine = table_ref[0], table_ref[1]
        minus = -sine
        fwd[:n, :n] = cosine
        fwd[:n, n:] = minus
        fwd[n:, :n] = sine
        fwd[n:, n:] = cosine
        adj[:n, :n] = cosine
        adj[:n, n:] = sine
        adj[n:, :n] = minus
        adj[n:, n:] = cosine

    r = off_ref[k, 0]
    c = off_ref[k, 1]
    fine = lax.rem(r, 8)
    base = pl.multiple_of(r - fine, 8)
    for d in range(2):
        x = pltpu.roll(ext[d, pl.ds(base, n + 8), :], lax.rem(width - c, width), 1)[:, :n]
        win[d] = pltpu.roll(x, lax.rem(n + 8 - fine, n + 8), 0)[:n]
    pg_ref[4] += win[0] * win[0] + win[1] * win[1]
    for m in range(2):
        p_re, p_im = probe_ref[m, 0], probe_ref[m, 1]
        o_re, o_im = win[0], win[1]
        wave[m * n : (m + 1) * n, :n] = (p_re * o_re - p_im * o_im).astype(BF16)
        wave[m * n : (m + 1) * n, n:] = (p_re * o_im + p_im * o_re).astype(BF16)
    half = jnp.dot(wave[...], fwd[...], preferred_element_type=F32).astype(BF16)
    for m in range(2):
        for d in range(2):
            mid[d * n : (d + 1) * n, m * n : (m + 1) * n] = half[m * n : (m + 1) * n, d * n : (d + 1) * n]
    far[...] = jnp.dot(adj[...], mid[...], preferred_element_type=F32)
    power = jnp.zeros((n, n), F32)
    for e in range(2):
        for m in range(2):
            f = far[e * n : (e + 1) * n, m * n : (m + 1) * n]
            power = power + f * f
    magnitude = jnp.sqrt(power)
    amplitude = amp_ref[0]
    miss = magnitude - amplitude
    loss_ref[...] += jnp.sum((miss * miss).reshape(n // 8, 8, n), 0)
    weight = 0.25 * (1.0 - amplitude / jnp.maximum(magnitude, 0.5))
    for e in range(2):
        for m in range(2):
            part = (slice(e * n, (e + 1) * n), slice(m * n, (m + 1) * n))
            mid[part] = (weight * far[part]).astype(BF16)
    half = jnp.dot(fwd[...], mid[...], preferred_element_type=F32).astype(BF16)
    for m in range(2):
        for d in range(2):
            wave[m * n : (m + 1) * n, d * n : (d + 1) * n] = half[d * n : (d + 1) * n, m * n : (m + 1) * n]
    far[...] = jnp.dot(wave[...], adj[...], preferred_element_type=F32)
    w_re = jnp.zeros((n, n), F32)
    w_im = jnp.zeros((n, n), F32)
    for m in range(2):
        g_re, g_im = far[m * n : (m + 1) * n, :n], far[m * n : (m + 1) * n, n:]
        p_re, p_im = probe_ref[m, 0], probe_ref[m, 1]
        o_re, o_im = win[0], win[1]
        w_re = w_re + p_re * g_re + p_im * g_im
        w_im = w_im + p_re * g_im - p_im * g_re
        pg_ref[2 * m] += o_re * g_re + o_im * g_im
        pg_ref[2 * m + 1] += o_re * g_im - o_im * g_re
    for d, v in ((0, w_re), (1, w_im)):
        v = pltpu.roll(jnp.concatenate([v, jnp.zeros((8, n), F32)], 0), fine, 0)
        v = jnp.concatenate([v, jnp.zeros((n + 8, width - n), F32)], 1)
        grad_ref[d, pl.ds(base, n + 8), :] += pltpu.roll(v, c, 1)

    if not first:

        @pl.when(k == pl.num_programs(0) - 1)
        def _():
            shards = payload_ref.shape[0]
            rows = n // shards
            for s in range(shards):
                for q in range(5):
                    payload_ref[s, q * rows : (q + 1) * rows] = pg_ref[q, s * rows : (s + 1) * rows]
                payload_ref[s, 5 * rows :] = loss_ref[...]


def windows(first, shards, offs, top, bottom, top_block, bottom_block, probe, amplitude, amp_first, table, carried=()):
    count = offs.shape[0]
    n = probe.shape[-1]
    rows, width = n, top.shape[2]

    def whole(*shape):
        return pl.BlockSpec(shape, lambda k, o: (0,) * len(shape))

    in_specs = [
        pl.BlockSpec((2, rows, width), lambda k, o: (0, top_block, 0)),
        pl.BlockSpec((2, rows, width), lambda k, o: (0, bottom_block, 0)),
        whole(*probe.shape),
        pl.BlockSpec((1, n, n), lambda k, o: (amp_first + k, 0, 0)),
        whole(*table.shape),
    ]
    out_specs = [whole(2, 2 * rows, width)]
    out_shape = [jax.ShapeDtypeStruct((2, 2 * rows, width), F32)]
    scratch = []
    if first:
        out_specs += [whole(5, n, n), whole(8, n)]
        out_shape += [jax.ShapeDtypeStruct((5, n, n), F32), jax.ShapeDtypeStruct((8, n), F32)]
    else:
        in_specs += [whole(5, n, n), whole(8, n)]
        shape = (shards, 5 * (n // shards) + 8, n)
        out_specs += [whole(*shape)]
        out_shape += [jax.ShapeDtypeStruct(shape, F32)]
        scratch += [pltpu.VMEM((5, n, n), F32), pltpu.VMEM((8, n), F32)]
    scratch += [
        pltpu.VMEM((2, 2 * rows, width), F32),
        pltpu.VMEM((2, n, n), F32),
        pltpu.VMEM((2 * n, 2 * n), BF16),
        pltpu.VMEM((2 * n, 2 * n), BF16),
        pltpu.VMEM((2 * n, 2 * n), F32),
        pltpu.VMEM((2 * n, 2 * n), BF16),
        pltpu.VMEM((2 * n, 2 * n), BF16),
    ]
    return pl.pallas_call(
        functools.partial(windows_kernel, first),
        grid_spec=pltpu.PrefetchScalarGridSpec(
            num_scalar_prefetch=1,
            grid=(count,),
            in_specs=in_specs,
            out_specs=out_specs,
            scratch_shapes=scratch,
        ),
        out_shape=out_shape,
        compiler_params=pltpu.CompilerParams(vmem_limit_bytes=52 << 20),
        name="near" if first else "across",
    )(offs, top, bottom, probe, amplitude, table, *carried)


def swap(x, bit):
    size = lax.axis_size("row")
    return lax.ppermute(x, "row", [(i, i ^ bit) for i in range(size)])


def per_device(object_field, probe, amplitude, offsets):
    tile = object_field.shape[1]
    n = probe.shape[2]
    count = offsets.shape[0]
    near = count // 2
    size = lax.axis_size("row")
    me = lax.axis_index("row")
    table = jnp.asarray(dft_tables(n))
    below = lax.ppermute(object_field[:, :n], "row", [(i, i - 1) for i in range(1, size)])
    offs = offsets - jnp.stack([me * tile, 0])
    grad_a, pg, loss = windows(
        True, size, offs[:near], object_field, object_field, 0, 1, probe, amplitude, 0, table
    )
    grad_b, x = windows(
        False,
        size,
        offs[near:] - jnp.array([n, 0], jnp.int32),
        object_field,
        below,
        1,
        0,
        probe,
        amplitude,
        near,
        table,
        (pg, loss),
    )
    carried = lax.ppermute(grad_b[:, n:], "row", [(i, i + 1) for i in range(size - 1)])
    bits = [1 << b for b in range(size.bit_length() - 1)]
    order = bits[:2] + bits[2:][::-1]
    for bit in order:
        half = x.shape[0] // 2
        mine = (me // bit) % 2
        keep = jnp.where(mine == 0, x[:half], x[half:])
        send = jnp.where(mine == 0, x[half:], x[:half])
        x = keep + swap(send, bit)
    rows = n // size
    x = x[0]
    loss = jnp.sum(x[5 * rows :]) / (count * size * n * n)
    y = x[: 4 * rows].reshape(4, rows, n) / jnp.sqrt(x[4 * rows : 5 * rows] + 1.0)
    y = y[None]
    for bit in order[::-1]:
        other = swap(y, bit)
        mine = (me // bit) % 2
        y = jnp.where(mine == 0, jnp.concatenate([y, other]), jnp.concatenate([other, y]))
    probe_dir = jnp.transpose(y, (1, 0, 2, 3)).reshape(2, 2, n, n)
    object_grad = jnp.concatenate([grad_a[:, :n] + carried, grad_a[:, n:] + grad_b[:, :n]], 1)
    return (object_grad, probe_dir, loss.reshape(1))


def solution(mesh):
    placed = (
        P(None, ("groups", "row"), None),
        P(),
        P(("groups", "row"), None, None),
        P(("groups", "row"), None),
    )
    return jax.shard_map(
        per_device,
        mesh=mesh,
        in_specs=placed,
        out_specs=(P(None, ("groups", "row"), None), P("groups", None, None, None), P("groups")),
        check_vma=False,
    )
```

```python
import functools
import math

import jax
import jax.numpy as jnp
import ml_dtypes
import numpy as np
from jax import lax
from jax.experimental import pallas as pl
from jax.experimental.pallas import tpu as pltpu
from jax.sharding import PartitionSpec as P

F32, BF16 = jnp.float32, jnp.bfloat16


def dft_tables(size):
    idx = np.arange(size)
    angle = (idx[:, None] * idx[None, :] % size).astype(np.float32) * np.float32(2.0 * math.pi / size)
    scale = np.float32(1.0 / math.sqrt(size))
    return np.stack([np.cos(angle) * scale, np.sin(angle) * scale]).astype(ml_dtypes.bfloat16)


def windows_kernel(first, off_ref, *refs):
    if first:
        top_ref, bottom_ref, probe_ref, amp_ref, table_ref = refs[:5]
        refs = refs[5:]
        grad_ref, pg_ref, loss_ref = refs[:3]
    else:
        top_ref, bottom_ref, probe_ref, amp_ref, table_ref, pg_in, loss_in = refs[:7]
        refs = refs[7:]
        grad_ref, slots = refs[0], refs[1:4]
        pg_ref, loss_ref = refs[4:6]
    ext, win, wave, mid, far, fwd, adj = refs[-7:]
    shards, rows = pg_ref.shape[1:3]
    k = pl.program_id(0)
    n = probe_ref.shape[-1]
    half_rows = top_ref.shape[1]
    width = ext.shape[2]

    @pl.when(k == 0)
    def _():
        grad_ref[...] = jnp.zeros_like(grad_ref)
        if first:
            pg_ref[...] = jnp.zeros_like(pg_ref)
            loss_ref[...] = jnp.zeros_like(loss_ref)
        else:
            pg_ref[...] = pg_in[...]
            loss_ref[...] = loss_in[...]
        ext[:, :half_rows] = top_ref[...]
        ext[:, half_rows:] = bottom_ref[...]
        cosine, sine = table_ref[0], table_ref[1]
        minus = -sine
        fwd[:n, :n] = cosine
        fwd[:n, n:] = minus
        fwd[n:, :n] = sine
        fwd[n:, n:] = cosine
        adj[:n, :n] = cosine
        adj[:n, n:] = sine
        adj[n:, :n] = minus
        adj[n:, n:] = cosine

    r = off_ref[k, 0]
    c = off_ref[k, 1]
    fine = lax.rem(r, 8)
    base = pl.multiple_of(r - fine, 8)
    for d in range(2):
        x = pltpu.roll(ext[d, pl.ds(base, n + 8), :], lax.rem(width - c, width), 1)[:, :n]
        win[d] = pltpu.roll(x, lax.rem(n + 8 - fine, n + 8), 0)[:n]
    pg_ref[4] += (win[0] * win[0] + win[1] * win[1]).reshape(shards, rows, n)
    for m in range(2):
        p_re, p_im = probe_ref[m, 0], probe_ref[m, 1]
        o_re, o_im = win[0], win[1]
        wave[m * n : (m + 1) * n, :n] = (p_re * o_re - p_im * o_im).astype(BF16)
        wave[m * n : (m + 1) * n, n:] = (p_re * o_im + p_im * o_re).astype(BF16)
    half = jnp.dot(wave[...], fwd[...], preferred_element_type=F32).astype(BF16)
    for m in range(2):
        for d in range(2):
            mid[d * n : (d + 1) * n, m * n : (m + 1) * n] = half[m * n : (m + 1) * n, d * n : (d + 1) * n]
    far[...] = jnp.dot(adj[...], mid[...], preferred_element_type=F32)
    power = jnp.zeros((n, n), F32)
    for e in range(2):
        for m in range(2):
            f = far[e * n : (e + 1) * n, m * n : (m + 1) * n]
            power = power + f * f
    magnitude = jnp.sqrt(power)
    amplitude = amp_ref[0]
    miss = magnitude - amplitude
    loss_ref[...] += jnp.sum((miss * miss).reshape(n // 8, 8, n), 0)
    weight = 0.25 * (1.0 - amplitude / jnp.maximum(magnitude, 0.5))
    for e in range(2):
        for m in range(2):
            part = (slice(e * n, (e + 1) * n), slice(m * n, (m + 1) * n))
            mid[part] = (weight * far[part]).astype(BF16)
    half = jnp.dot(fwd[...], mid[...], preferred_element_type=F32).astype(BF16)
    for m in range(2):
        for d in range(2):
            wave[m * n : (m + 1) * n, d * n : (d + 1) * n] = half[d * n : (d + 1) * n, m * n : (m + 1) * n]
    far[...] = jnp.dot(wave[...], adj[...], preferred_element_type=F32)
    w_re = jnp.zeros((n, n), F32)
    w_im = jnp.zeros((n, n), F32)
    for m in range(2):
        g_re, g_im = far[m * n : (m + 1) * n, :n], far[m * n : (m + 1) * n, n:]
        p_re, p_im = probe_ref[m, 0], probe_ref[m, 1]
        o_re, o_im = win[0], win[1]
        w_re = w_re + p_re * g_re + p_im * g_im
        w_im = w_im + p_re * g_im - p_im * g_re
        pg_ref[2 * m] += (o_re * g_re + o_im * g_im).reshape(shards, rows, n)
        pg_ref[2 * m + 1] += (o_re * g_im - o_im * g_re).reshape(shards, rows, n)
    for d, v in ((0, w_re), (1, w_im)):
        v = pltpu.roll(jnp.concatenate([v, jnp.zeros((8, n), F32)], 0), fine, 0)
        v = jnp.concatenate([v, jnp.zeros((n + 8, width - n), F32)], 1)
        grad_ref[d, pl.ds(base, n + 8), :] += pltpu.roll(v, c, 1)

    if not first:

        @pl.when(k == pl.num_programs(0) - 1)
        def _():
            me = off_ref[off_ref.shape[0] - 1, 0]
            loss = loss_ref[:, : n // 2] + loss_ref[:, n // 2 :]
            for d in range(shards):
                part = slot_of(d, shards)
                size = shards // 2
                ref, part = (slots[0], part - size) if part >= size else (slots[2 - part // (size // 2)], part % (size // 2))
                owner = me ^ d
                for q in range(5):
                    value = pg_ref[q, owner]
                    ref[part, 2 * q * rows : (2 * q + 1) * rows] = value[:, : n // 2]
                    ref[part, (2 * q + 1) * rows : (2 * q + 2) * rows] = value[:, n // 2 :]
                ref[part, 10 * rows :] = loss


def slot_of(d, shards):
    return (d & 1) * (shards // 2) + (d >> 1 & 1) * (shards // 4) + (d >> 2)


def assemble_kernel(me_ref, own_ref, other_ref, out_ref):
    half, planes, rows, n = own_ref.shape
    shards = 2 * half
    for d in range(shards):
        part = slot_of(d, shards)
        ref, part = (other_ref, part - half) if part >= half else (own_ref, part)
        for q in range(planes):
            out_ref[q, me_ref[0] ^ d] = ref[part, q]


def windows(first, shards, count, offs, top, bottom, top_block, bottom_block, probe, amplitude, amp_first, table, carried=()):
    n = probe.shape[-1]
    rows, width = n, top.shape[2]
    sums = (5, shards, n // shards, n)

    def whole(*shape):
        return pl.BlockSpec(shape, lambda k, o: (0,) * len(shape))

    in_specs = [
        pl.BlockSpec((2, rows, width), lambda k, o: (0, top_block, 0)),
        pl.BlockSpec((2, rows, width), lambda k, o: (0, bottom_block, 0)),
        whole(*probe.shape),
        pl.BlockSpec((1, n, n), lambda k, o: (amp_first + k, 0, 0)),
        whole(*table.shape),
    ]
    out_specs = [whole(2, 2 * rows, width)]
    out_shape = [jax.ShapeDtypeStruct((2, 2 * rows, width), F32)]
    scratch = []
    if first:
        out_specs += [whole(*sums), whole(8, n)]
        out_shape += [jax.ShapeDtypeStruct(sums, F32), jax.ShapeDtypeStruct((8, n), F32)]
    else:
        in_specs += [whole(*sums), whole(8, n)]
        for count_of in (shards // 2, shards // 4, shards // 4):
            shape = (count_of, 10 * (n // shards) + 8, n // 2)
            out_specs += [whole(*shape)]
            out_shape += [jax.ShapeDtypeStruct(shape, F32)]
        scratch += [pltpu.VMEM(sums, F32), pltpu.VMEM((8, n), F32)]
    scratch += [
        pltpu.VMEM((2, 2 * rows, width), F32),
        pltpu.VMEM((2, n, n), F32),
        pltpu.VMEM((2 * n, 2 * n), BF16),
        pltpu.VMEM((2 * n, 2 * n), BF16),
        pltpu.VMEM((2 * n, 2 * n), F32),
        pltpu.VMEM((2 * n, 2 * n), BF16),
        pltpu.VMEM((2 * n, 2 * n), BF16),
    ]
    return pl.pallas_call(
        functools.partial(windows_kernel, first),
        grid_spec=pltpu.PrefetchScalarGridSpec(
            num_scalar_prefetch=1,
            grid=(count,),
            in_specs=in_specs,
            out_specs=out_specs,
            scratch_shapes=scratch,
        ),
        out_shape=out_shape,
        compiler_params=pltpu.CompilerParams(vmem_limit_bytes=52 << 20),
        name="near" if first else "across",
    )(offs, top, bottom, probe, amplitude, table, *carried)


def assemble(me, own, other):
    half, planes, rows, n = own.shape
    whole = pl.BlockSpec(memory_space=pltpu.VMEM)
    return pl.pallas_call(
        assemble_kernel,
        in_specs=[pl.BlockSpec(memory_space=pltpu.SMEM), whole, whole],
        out_specs=whole,
        out_shape=jax.ShapeDtypeStruct((planes, 2 * half, rows, n), F32),
        name="assemble",
    )(me.reshape(1), own, other)


def swap(x, bit):
    size = lax.axis_size("row")
    return lax.ppermute(x, "row", [(i, i ^ bit) for i in range(size)])


def per_device(object_field, probe, amplitude, offsets):
    tile = object_field.shape[1]
    n = probe.shape[2]
    count = offsets.shape[0]
    near = count // 2
    size = lax.axis_size("row")
    me = lax.axis_index("row")
    table = jnp.asarray(dft_tables(n))
    below = lax.ppermute(object_field[:, :n], "row", [(i, i - 1) for i in range(1, size)])
    offs = offsets - jnp.stack([me * tile, 0])
    grad_a, pg, loss = windows(
        True, size, near, offs[:near], object_field, object_field, 0, 1, probe, amplitude, 0, table
    )
    grad_b, away, beside, x = windows(
        False,
        size,
        count - near,
        jnp.concatenate([offs[near:] - jnp.array([n, 0], jnp.int32), jnp.stack([me, 0])[None]]),
        object_field,
        below,
        1,
        0,
        probe,
        amplitude,
        near,
        table,
        (pg, loss),
    )
    carried = lax.ppermute(grad_b[:, n:], "row", [(i, i + 1) for i in range(size - 1)])
    quarter = size // 4
    away = swap(away, 1)
    beside = swap(beside + away[quarter:], 2)
    x = x + away[:quarter] + beside
    parts = [x[0]] + [swap(x[z], 4 * z) for z in range(1, quarter)]
    while len(parts) > 1:
        parts = [a + b for a, b in zip(parts[::2], parts[1::2])]
    total = parts[0]
    rows = n // size
    loss = jnp.sum(total[10 * rows :]) / (count * size * n * n)
    planes = total[: 10 * rows].reshape(5, 2, rows, n // 2)
    y = planes[:4] / jnp.sqrt(planes[4] + 1.0)
    y = jnp.concatenate([y[:, 0], y[:, 1]], -1)
    y = jnp.stack([y] + [swap(y, 4 * z) for z in range(1, quarter)])
    y = jnp.concatenate([y, swap(y, 2)])
    probe_dir = assemble(me, y, swap(y, 1)).reshape(2, 2, n, n)
    object_grad = jnp.concatenate([grad_a[:, :n] + carried, grad_a[:, n:] + grad_b[:, :n]], 1)
    return (object_grad, probe_dir, loss.reshape(1))


def solution(mesh):
    placed = (
        P(None, ("groups", "row"), None),
        P(),
        P(("groups", "row"), None, None),
        P(("groups", "row"), None),
    )
    return jax.shard_map(
        per_device,
        mesh=mesh,
        in_specs=placed,
        out_specs=(P(None, ("groups", "row"), None), P("groups", None, None, None), P("groups")),
        check_vma=False,
    )
```

```python
import functools
import math

import jax
import jax.numpy as jnp
import ml_dtypes
import numpy as np
from jax import lax
from jax.experimental import pallas as pl
from jax.experimental.pallas import tpu as pltpu
from jax.sharding import PartitionSpec as P

F32, BF16 = jnp.float32, jnp.bfloat16
LANES = 128
GROUP = 2
VMEM_MIB = 30


def dft_tables(n):
    h = n // 2
    idx = np.arange(n)
    angle = (idx[:, None] * idx[None, :] % n).astype(np.float32) * np.float32(2.0 * math.pi / n)
    scale = np.float32(1.0 / math.sqrt(n))
    c, s = np.cos(angle) * scale, np.sin(angle) * scale
    near = np.arange(h)
    even, odd = 2 * near, 2 * near + 1
    turned = 2 * ((near + h // 2) % h) + 1

    def column(k):
        a, b = c[np.ix_(near, k)], s[np.ix_(near, k)]
        return np.block([[a, -b], [b, a]])

    def row(r):
        a, b = c[np.ix_(r, near)], s[np.ix_(r, near)]
        return np.block([[a, b], [-b, a]])

    tables = [column(even), column(turned), row(even), row(odd)]
    return np.stack(tables + [tables[1].T, tables[3].T]).astype(ml_dtypes.bfloat16)


def windows_kernel(first, amp_first, off_ref, *refs):
    object_ref, probe_hbm, amp_hbm, tab_hbm = refs[:4]
    if first:
        grad_out, pg_out, loss_out = refs[4:7]
    else:
        below_ref, grad_in, pg_in, loss_in, grad_out, low_out, keep_out, away_out, keep_ref, away_ref = refs[4:14]
    ext, grad, pg_ref, loss_ref, probe_ref, tab, amp_s, win_s, lhs_s, hs_s, far_s, sems = refs[-12:]
    shards, rows = pg_ref.shape[1:3]
    k = pl.program_id(0)
    n = probe_ref.shape[-1]
    h = n // 2
    width = ext.shape[2]
    below_row = 0 if first else n
    lane = lax.broadcasted_iota(jnp.int32, (1, 1, LANES), 2)
    sub = lax.broadcasted_iota(jnp.int32, (1, 8, 1), 1)

    def amplitude_copies(group):
        at = amp_first + group * GROUP
        return [
            pltpu.make_async_copy(
                amp_hbm.at[pl.ds(at, GROUP), :, pl.ds(q * LANES, LANES)], amp_s.at[group, q], sems.at[8 + 2 * group + q]
            )
            for q in range(2)
        ]

    if first:
        windows_in = [(object_ref, ext)]
        sums_in = []
    else:
        windows_in = [(object_ref.at[:, pl.ds(n, n)], ext.at[:, pl.ds(0, n)]), (below_ref, ext.at[:, pl.ds(n, n)])]
        sums_in = [(grad_in, grad.at[:, pl.ds(0, 2 * n)]), (pg_in, pg_ref), (loss_in, loss_ref)]
    windows_in = [*windows_in, (probe_hbm, probe_ref)]
    windows_in = [pltpu.make_async_copy(a, b, sems.at[i]) for i, (a, b) in enumerate(windows_in)]
    table_in = pltpu.make_async_copy(tab_hbm, tab, sems.at[3])
    sums_in = [pltpu.make_async_copy(a, b, sems.at[4 + i]) for i, (a, b) in enumerate(sums_in)]

    @pl.when(k == 0)
    def _():
        for copy in (*windows_in, table_in, *amplitude_copies(0), *amplitude_copies(1), *sums_in):
            copy.start()
        if first:
            grad[...] = jnp.zeros_like(grad)
            pg_ref[...] = jnp.zeros_like(pg_ref)
            loss_ref[...] = jnp.zeros_like(loss_ref)
        else:
            grad[:, 2 * n :] = jnp.zeros((2, n, width), F32)
        for copy in (*windows_in, table_in, *sums_in):
            copy.wait()

    for copy in amplitude_copies(k):
        copy.wait()

    def dot(a, b):
        return jnp.dot(a, b, preferred_element_type=F32)

    places = []
    for g in range(GROUP):
        r, c = off_ref[amp_first + k * GROUP + g, 0] - below_row, off_ref[amp_first + k * GROUP + g, 1]
        fine = lax.rem(r, 8)
        places.append((pl.multiple_of(r - fine, 8), fine, c))

    def load(g):
        base, fine, c = places[g]
        win = win_s.at[g]
        in_lane, in_sub = lane < LANES - c, sub < 8 - fine
        back_lane, back_sub = lax.rem(LANES - c, LANES), lax.rem(8 - fine, 8)
        for d in range(2):
            x = ext[d, pl.ds(base, n + 8), :].reshape(n // 8 + 1, 8, width)
            t = [pltpu.roll(x[:, :, LANES * q : LANES * (q + 1)], back_lane, 2) for q in range(3)]
            for q in range(2):
                y = pltpu.roll(jnp.where(in_lane, t[q], t[q + 1]), back_sub, 1)
                win[d, :, LANES * q : LANES * (q + 1)] = jnp.where(in_sub, y[:-1], y[1:]).reshape(n, LANES)

    def wave(g):
        win, lhs = win_s.at[g], lhs_s.at[g]
        for m in range(2):
            parts = []
            for j in range(2):
                js = slice(j * h, (j + 1) * h)
                p_re, p_im = probe_ref[m, 0, :, js], probe_ref[m, 1, :, js]
                o_re, o_im = win[0, :, js], win[1, :, js]
                parts.append((p_re * o_re - p_im * o_im, p_re * o_im + p_im * o_re))
            for d in range(2):
                at = (slice(m * n, (m + 1) * n), slice(d * h, (d + 1) * h))
                lhs[(0, *at)] = (parts[0][d] + parts[1][d]).astype(BF16)
                lhs[(1, *at)] = (parts[0][d] - parts[1][d]).astype(BF16)

    def columns(g):
        lhs, hs = lhs_s.at[g], hs_s.at[g]
        for p in range(2):
            v = dot(lhs[p], tab[p])
            for m in range(2):
                top, bottom = v[m * n : m * n + h], v[m * n + h : (m + 1) * n]
                for u, z in ((0, top + bottom), (1, top - bottom)):
                    for d in range(2):
                        at = (u, slice(d * h, (d + 1) * h), slice((2 * m + p) * h, (2 * m + p + 1) * h))
                        hs[at] = z[:, d * h : (d + 1) * h].astype(BF16)

    def down(g):
        hs, far = hs_s.at[g], far_s.at[g]
        for u in range(2):
            far[u] = dot(tab[2 + u], hs[u])

    idx = lax.broadcasted_iota(jnp.int32, (h, LANES), 1)
    lower = idx < LANES // 2
    pick_lo = jnp.where(lower, 2 * idx, 2 * idx - (LANES - 1))
    pick_hi = jnp.where(lower, 2 * idx + 1, 2 * idx - LANES)

    def weigh(g):
        hs, far = hs_s.at[g], far_s.at[g]
        total = jnp.zeros((8, n), F32)
        for u in range(2):
            lo = jnp.take_along_axis(amp_s[k, 0, g, pl.ds(u, h, stride=2), :], pick_lo, 1)
            hi = jnp.take_along_axis(amp_s[k, 1, g, pl.ds(u, h, stride=2), :], pick_hi, 1)
            amplitude = jnp.concatenate([jnp.where(lower, lo, hi), jnp.where(lower, hi, lo)], 1)
            power = None
            for e in range(2):
                for m in range(2):
                    f = far[u, e * h : (e + 1) * h, m * n : (m + 1) * n]
                    power = f * f if power is None else power + f * f
            magnitude = jnp.sqrt(power)
            miss = magnitude - amplitude
            total = total + jnp.sum((miss * miss).reshape(h // 8, 8, n), 0)
            weight = 0.25 * (1.0 - amplitude / jnp.maximum(magnitude, 0.5))
            for e in range(2):
                for m in range(2):
                    at = (u, slice(e * h, (e + 1) * h), slice(m * n, (m + 1) * n))
                    hs[at] = (weight * far[at]).astype(BF16)
        loss_ref[...] += total

    def up(g):
        lhs, hs = lhs_s.at[g], hs_s.at[g]
        a, b = dot(tab[0], hs[0]), dot(tab[5], hs[1])
        for j, z in ((0, a + b), (1, a - b)):
            for m in range(2):
                for p in range(2):
                    for d in range(2):
                        at = (p, slice(m * n + j * h, m * n + (j + 1) * h), slice(d * h, (d + 1) * h))
                        lhs[at] = z[d * h : (d + 1) * h, (2 * m + p) * h : (2 * m + p + 1) * h].astype(BF16)

    def columns_back(g):
        lhs, far = lhs_s.at[g], far_s.at[g]
        a, b = dot(lhs[0], tab[2]), dot(lhs[1], tab[4])
        for j, z in ((0, a + b), (1, a - b)):
            far[j] = jnp.concatenate([z[:n], z[n:]], 1)

    def sums():
        for j in range(2):
            js = slice(j * h, (j + 1) * h)
            for m in range(2):
                s_re = s_im = None
                for g in range(GROUP):
                    g_re, g_im = far_s[g, j, :, m * n : m * n + h], far_s[g, j, :, m * n + h : (m + 1) * n]
                    o_re, o_im = win_s[g, 0, :, js], win_s[g, 1, :, js]
                    a, b = o_re * g_re + o_im * g_im, o_re * g_im - o_im * g_re
                    s_re, s_im = (a, b) if s_re is None else (s_re + a, s_im + b)
                pg_ref[2 * m, :, :, js] += s_re.reshape(shards, rows, h)
                pg_ref[2 * m + 1, :, :, js] += s_im.reshape(shards, rows, h)
            s = None
            for g in range(GROUP):
                o_re, o_im = win_s[g, 0, :, js], win_s[g, 1, :, js]
                v = o_re * o_re + o_im * o_im
                s = v if s is None else s + v
            pg_ref[4, :, :, js] += s.reshape(shards, rows, h)

    def scatter(g):
        base, fine, c = places[g]
        far = far_s.at[g]
        from_sub, from_lane = sub >= fine, lane >= c
        t = [[], []]
        for j in range(2):
            js = slice(j * h, (j + 1) * h)
            w = [None, None]
            for m in range(2):
                g_re, g_im = far[j, :, m * n : m * n + h], far[j, :, m * n + h : (m + 1) * n]
                p_re, p_im = probe_ref[m, 0, :, js], probe_ref[m, 1, :, js]
                v = (p_re * g_re + p_im * g_im, p_re * g_im - p_im * g_re)
                w = [x if y is None else x + y for x, y in zip(v, w)]
            for d in range(2):
                y = pltpu.roll(w[d].reshape(n // 8, 8, LANES), fine, 1)
                z = jnp.zeros((1, 8, LANES), F32)
                y = jnp.where(from_sub, jnp.concatenate([y, z], 0), jnp.concatenate([z, y], 0))
                t[d].append(pltpu.roll(y, c, 2))
        for d in range(2):
            a, b = t[d]
            out = [jnp.where(from_lane, a, 0.0), jnp.where(from_lane, b, a), jnp.where(from_lane, 0.0, b)]
            for q in range(3):
                grad[d, pl.ds(base + below_row, n + 8), LANES * q : LANES * (q + 1)] += out[q].reshape(n + 8, LANES)

    for stage in (load, wave, columns, down, weigh, up, columns_back):
        for g in range(GROUP):
            stage(g)
    sums()
    for g in range(GROUP):
        scatter(g)

    @pl.when(k == pl.num_programs(0) - 1)
    def _():
        if first:
            out = [(grad, grad_out), (pg_ref, pg_out), (loss_ref, loss_out)]
            out = [pltpu.make_async_copy(a, b, sems.at[i]) for i, (a, b) in enumerate(out)]
            for copy in out:
                copy.start()
            for copy in out:
                copy.wait()
            return
        out = [(grad.at[:, pl.ds(2 * n, n)], low_out), (grad.at[:, pl.ds(0, 2 * n)], grad_out), (away_ref, away_out), (keep_ref, keep_out)]
        out = [pltpu.make_async_copy(a, b, sems.at[i]) for i, (a, b) in enumerate(out)]
        out[0].start()
        out[1].start()
        me = off_ref[off_ref.shape[0] - 1, 0]
        loss = loss_ref[:, : n // 2] + loss_ref[:, n // 2 :]
        for core in (1, 0):
            ref = away_ref if core else keep_ref
            for slot in range(shards // 2):
                owner = owner_of(me, core, slot, shards)
                for q in range(5):
                    value = pg_ref[q, owner]
                    ref[slot, 2 * q * rows : (2 * q + 1) * rows] = value[:, : n // 2]
                    ref[slot, (2 * q + 1) * rows : (2 * q + 2) * rows] = value[:, n // 2 :]
                ref[slot, 10 * rows :] = loss
            out[3 - core].start()
        for copy in out:
            copy.wait()


def owner_of(me, core, slot, size):
    z = lax.rem(me // 4 + slot % (size // 4), size // 4)
    return z * 4 + ((me & 3) ^ (core + 2 * (slot // (size // 4))))


def windows(first, shards, count, offs, object_field, probe, amplitude, amp_first, table, carried=()):
    n = probe.shape[-1]
    width = object_field.shape[2]
    sums = (5, shards, n // shards, n)
    hbm, anywhere = pl.BlockSpec(memory_space=pltpu.HBM), pl.BlockSpec(memory_space=pl.ANY)
    inputs = (object_field, probe, amplitude, table, *carried)
    scratch = []
    if first:
        shapes = [(2, 2 * n, width), sums, (8, n)]
    else:
        slots = (shards // 2, 10 * (n // shards) + 8, n // 2)
        shapes = [(2, 2 * n, width), (2, n, width), slots, slots]
        scratch += [pltpu.VMEM(slots, F32)] * 2
    scratch += [
        pltpu.VMEM((2, 2 * n, width), F32),
        pltpu.VMEM((2, 2 * n if first else 3 * n, width), F32),
        pltpu.VMEM(sums, F32),
        pltpu.VMEM((8, n), F32),
        pltpu.VMEM(probe.shape, F32),
        pltpu.VMEM(table.shape, BF16),
        pltpu.VMEM((count // GROUP, 2, GROUP, n, LANES), F32),
        pltpu.VMEM((GROUP, 2, n, n), F32),
        pltpu.VMEM((GROUP, 2, 2 * n, n), BF16),
        pltpu.VMEM((GROUP, 2, n, 2 * n), BF16),
        pltpu.VMEM((GROUP, 2, n, 2 * n), F32),
        pltpu.SemaphoreType.DMA((12,)),
    ]
    return pl.pallas_call(
        functools.partial(windows_kernel, first, amp_first),
        grid_spec=pltpu.PrefetchScalarGridSpec(
            num_scalar_prefetch=1,
            grid=(count // GROUP,),
            in_specs=[anywhere] * len(inputs),
            out_specs=[anywhere] * len(shapes),
            scratch_shapes=scratch,
        ),
        out_shape=[jax.ShapeDtypeStruct(s, F32) for s in shapes],
        compiler_params=pltpu.CompilerParams(vmem_limit_bytes=VMEM_MIB << 20),
        name="near" if first else "across",
    )(offs, *inputs)


def assemble_kernel(scale, me_ref, own_ref, other_ref, losses_ref, out_ref, loss_ref, stage, sem):
    half, planes, rows, n = own_ref.shape
    quarter = losses_ref.shape[0]
    me = me_ref[0]
    copies = []
    for core, ref in enumerate((own_ref, other_ref)):
        for slot in range(half):
            owner = owner_of(me, core, slot, 2 * half)
            copies.append(pltpu.make_async_copy(ref.at[slot], stage.at[:, owner], sem.at[len(copies)]))
    for copy in copies:
        copy.start()
    loss = jnp.zeros(losses_ref.shape[1:], F32)
    for z in range(quarter):
        loss = loss + losses_ref[lax.rem(me // 4 + quarter - z, quarter)]
    loss_ref[0] = jnp.sum(loss) * scale
    for copy in copies:
        copy.wait()
    out = pltpu.make_async_copy(stage, out_ref, sem.at[0])
    out.start()
    out.wait()


def assemble(me, own, other, losses, scale):
    half, planes, rows, n = own.shape
    shape = (planes, 2 * half, rows, n)
    anywhere = pl.BlockSpec(memory_space=pl.ANY)
    return pl.pallas_call(
        functools.partial(assemble_kernel, scale),
        in_specs=[pl.BlockSpec(memory_space=pltpu.SMEM), anywhere, anywhere, pl.BlockSpec(memory_space=pltpu.VMEM)],
        out_specs=[pl.BlockSpec(memory_space=pltpu.HBM), pl.BlockSpec(memory_space=pltpu.SMEM)],
        out_shape=[jax.ShapeDtypeStruct(shape, F32), jax.ShapeDtypeStruct((1,), F32)],
        scratch_shapes=[pltpu.VMEM(shape, F32), pltpu.SemaphoreType.DMA((2 * half,))],
        name="assemble",
    )(me.reshape(1), own, other, losses)


def swap(x, bit):
    size = lax.axis_size("row")
    return lax.ppermute(x, "row", [(i, i ^ bit) for i in range(size)])


def shift(x, by):
    size = lax.axis_size("row")
    return lax.ppermute(x, "row", [(i, (i + by) % size) for i in range(size)])


def tree(parts):
    while len(parts) > 1:
        parts = [sum(parts[i + 1 : i + 2], parts[i]) for i in range(0, len(parts), 2)]
    return parts[0]


def per_device(object_field, probe, amplitude, offsets):
    tile = object_field.shape[1]
    n = probe.shape[2]
    count = offsets.shape[0]
    near = count // 2
    size = lax.axis_size("row")
    me = lax.axis_index("row")
    table = jnp.asarray(dft_tables(n))
    below = lax.ppermute(object_field[:, :n], "row", [(i, i - 1) for i in range(1, size)])
    offs = jnp.concatenate([offsets - jnp.stack([me * tile, 0]), jnp.stack([me, 0])[None]])
    grad, pg, loss = windows(True, size, near, offs, object_field, probe, amplitude, 0, table)
    grad, low, keep, away = windows(
        False, size, count - near, offs, object_field, probe, amplitude, near, table, (below, grad, pg, loss)
    )
    hop = lax.ppermute(low, "row", [(i, i + 4) for i in range(3, size - 4, 4)])
    rows = n // size
    quarter = size // 4
    away = swap(away, 1)
    beside = swap(keep[quarter:] + away[quarter:], 2)
    x = keep[:quarter] + away[:quarter] + beside
    hop, x = lax.optimization_barrier((hop, x))
    carried = jnp.where(me % 4 == 3, hop, low)
    carried = lax.ppermute(carried, "row", [(i, i - 3 if i % 4 == 3 else i + 1) for i in range(size)])
    parts = [x[0]] + [shift(x[z], 4 * z) for z in range(1, quarter)]
    total = tree(parts)
    losses = jnp.stack([p[10 * rows :] for p in parts])
    planes = total[: 10 * rows].reshape(5, 2, rows, n // 2)
    y = planes[:4] / jnp.sqrt(planes[4] + 1.0)
    y = jnp.concatenate([y[:, 0], y[:, 1]], -1)
    others = [shift(y, -4 * z) for z in range(1, quarter)]
    object_grad = grad.at[:, :n].add(carried)
    object_grad, y = lax.optimization_barrier((object_grad, y))
    y = jnp.stack([y] + others)
    y = jnp.concatenate([y, swap(y, 2)])
    probe_dir, loss = assemble(me, y, swap(y, 1), losses, 1.0 / (count * size * n * n))
    probe_dir = probe_dir.reshape(2, 2, n, n)
    return (object_grad, probe_dir, loss)


def solution(mesh):
    placed = (
        P(None, ("groups", "row"), None),
        P(),
        P(("groups", "row"), None, None),
        P(("groups", "row"), None),
    )
    return jax.shard_map(
        per_device,
        mesh=mesh,
        in_specs=placed,
        out_specs=(P(None, ("groups", "row"), None), P("groups", None, None, None), P("groups")),
        check_vma=False,
    )
```

```python
import functools
import math

import jax
import jax.numpy as jnp
import ml_dtypes
import numpy as np
from jax import lax
from jax.experimental import pallas as pl
from jax.experimental.pallas import tpu as pltpu
from jax.sharding import PartitionSpec as P

F32, BF16 = jnp.float32, jnp.bfloat16
LANES = 128
GROUP = 2
VMEM_MIB = 30


def dft_tables(n):
    h = n // 2
    idx = np.arange(n)
    angle = (idx[:, None] * idx[None, :] % n).astype(np.float32) * np.float32(2.0 * math.pi / n)
    scale = np.float32(1.0 / math.sqrt(n))
    c, s = np.cos(angle) * scale, np.sin(angle) * scale
    near = np.arange(h)
    even, odd = 2 * near, 2 * near + 1
    turned = 2 * ((near + h // 2) % h) + 1

    def column(k):
        a, b = c[np.ix_(near, k)], s[np.ix_(near, k)]
        return np.block([[a, -b], [b, a]])

    def row(r):
        a, b = c[np.ix_(r, near)], s[np.ix_(r, near)]
        return np.block([[a, b], [-b, a]])

    tables = [column(even), column(turned), row(even), row(odd)]
    return np.stack(tables + [tables[1].T, tables[3].T]).astype(ml_dtypes.bfloat16)


def windows_kernel(first, amp_first, off_ref, *refs):
    object_ref, probe_hbm, amp_hbm, tab_hbm = refs[:4]
    if first:
        grad_out, pg_out, loss_out = refs[4:7]
    else:
        below_ref, grad_in, pg_in, loss_in, grad_out, low_out, keep_out, away_out, keep_ref, away_ref = refs[4:14]
    ext, grad, pg_ref, loss_ref, probe_ref, tab, amp_s, win_s, lhs_s, hs_s, far_s, sems = refs[-12:]
    shards, rows = pg_ref.shape[1:3]
    k = pl.program_id(0)
    n = probe_ref.shape[-1]
    h = n // 2
    width = ext.shape[2]
    below_row = 0 if first else n
    lane = lax.broadcasted_iota(jnp.int32, (1, 1, LANES), 2)
    sub = lax.broadcasted_iota(jnp.int32, (1, 8, 1), 1)

    def amplitude_copies(group):
        at = amp_first + group * GROUP
        return [
            pltpu.make_async_copy(
                amp_hbm.at[pl.ds(at, GROUP), :, pl.ds(q * LANES, LANES)], amp_s.at[group, q], sems.at[8 + 2 * group + q]
            )
            for q in range(2)
        ]

    if first:
        windows_in = [(object_ref, ext)]
        sums_in = []
    else:
        windows_in = [(object_ref.at[:, pl.ds(n, n)], ext.at[:, pl.ds(0, n)]), (below_ref, ext.at[:, pl.ds(n, n)])]
        sums_in = [(grad_in, grad.at[:, pl.ds(0, 2 * n)]), (pg_in, pg_ref), (loss_in, loss_ref)]
    windows_in = [*windows_in, (probe_hbm, probe_ref)]
    windows_in = [pltpu.make_async_copy(a, b, sems.at[i]) for i, (a, b) in enumerate(windows_in)]
    table_in = pltpu.make_async_copy(tab_hbm, tab, sems.at[3])
    sums_in = [pltpu.make_async_copy(a, b, sems.at[4 + i]) for i, (a, b) in enumerate(sums_in)]

    @pl.when(k == 0)
    def _():
        for copy in (*windows_in, table_in, *amplitude_copies(0), *amplitude_copies(1), *sums_in):
            copy.start()
        if first:
            grad[...] = jnp.zeros_like(grad)
            pg_ref[...] = jnp.zeros_like(pg_ref)
            loss_ref[...] = jnp.zeros_like(loss_ref)
        else:
            grad[:, 2 * n :] = jnp.zeros((2, n, width), F32)
        for copy in (*windows_in, table_in, *sums_in):
            copy.wait()

    for copy in amplitude_copies(k):
        copy.wait()

    def dot(a, b):
        return jnp.dot(a, b, preferred_element_type=F32)

    places = []
    for g in range(GROUP):
        r, c = off_ref[amp_first + k * GROUP + g, 0] - below_row, off_ref[amp_first + k * GROUP + g, 1]
        fine = lax.rem(r, 8)
        places.append((pl.multiple_of(r - fine, 8), fine, c))

    def load(g):
        base, fine, c = places[g]
        win = win_s.at[g]
        in_lane, in_sub = lane < LANES - c, sub < 8 - fine
        back_lane, back_sub = lax.rem(LANES - c, LANES), lax.rem(8 - fine, 8)
        for d in range(2):
            x = ext[d, pl.ds(base, n + 8), :].reshape(n // 8 + 1, 8, width)
            t = [pltpu.roll(x[:, :, LANES * q : LANES * (q + 1)], back_lane, 2) for q in range(3)]
            for q in range(2):
                y = pltpu.roll(jnp.where(in_lane, t[q], t[q + 1]), back_sub, 1)
                win[d, :, LANES * q : LANES * (q + 1)] = jnp.where(in_sub, y[:-1], y[1:]).reshape(n, LANES)

    def wave(g):
        win, lhs = win_s.at[g], lhs_s.at[g]
        for m in range(2):
            parts = []
            for j in range(2):
                js = slice(j * h, (j + 1) * h)
                p_re, p_im = probe_ref[m, 0, :, js], probe_ref[m, 1, :, js]
                o_re, o_im = win[0, :, js], win[1, :, js]
                parts.append((p_re * o_re - p_im * o_im, p_re * o_im + p_im * o_re))
            for d in range(2):
                at = (slice(m * n, (m + 1) * n), slice(d * h, (d + 1) * h))
                lhs[(0, *at)] = (parts[0][d] + parts[1][d]).astype(BF16)
                lhs[(1, *at)] = (parts[0][d] - parts[1][d]).astype(BF16)

    def columns(g):
        lhs, hs = lhs_s.at[g], hs_s.at[g]
        for p in range(2):
            v = dot(lhs[p], tab[p])
            for m in range(2):
                top, bottom = v[m * n : m * n + h], v[m * n + h : (m + 1) * n]
                for u, z in ((0, top + bottom), (1, top - bottom)):
                    for d in range(2):
                        at = (u, slice(d * h, (d + 1) * h), slice((2 * m + p) * h, (2 * m + p + 1) * h))
                        hs[at] = z[:, d * h : (d + 1) * h].astype(BF16)

    def down(g):
        hs, far = hs_s.at[g], far_s.at[g]
        for u in range(2):
            far[u] = dot(tab[2 + u], hs[u])

    idx = lax.broadcasted_iota(jnp.int32, (h, LANES), 1)
    lower = idx < LANES // 2
    pick_lo = jnp.where(lower, 2 * idx, 2 * idx - (LANES - 1))
    pick_hi = jnp.where(lower, 2 * idx + 1, 2 * idx - LANES)

    def weigh(g):
        hs, far = hs_s.at[g], far_s.at[g]
        total = jnp.zeros((8, n), F32)
        for u in range(2):
            lo = jnp.take_along_axis(amp_s[k, 0, g, pl.ds(u, h, stride=2), :], pick_lo, 1)
            hi = jnp.take_along_axis(amp_s[k, 1, g, pl.ds(u, h, stride=2), :], pick_hi, 1)
            amplitude = jnp.concatenate([jnp.where(lower, lo, hi), jnp.where(lower, hi, lo)], 1)
            power = None
            for e in range(2):
                for m in range(2):
                    f = far[u, e * h : (e + 1) * h, m * n : (m + 1) * n]
                    power = f * f if power is None else power + f * f
            magnitude = jnp.sqrt(power)
            miss = magnitude - amplitude
            total = total + jnp.sum((miss * miss).reshape(h // 8, 8, n), 0)
            weight = 0.25 * (1.0 - amplitude / jnp.maximum(magnitude, 0.5))
            for e in range(2):
                for m in range(2):
                    at = (u, slice(e * h, (e + 1) * h), slice(m * n, (m + 1) * n))
                    hs[at] = (weight * far[at]).astype(BF16)
        loss_ref[...] += total

    def up(g):
        lhs, hs = lhs_s.at[g], hs_s.at[g]
        a, b = dot(tab[0], hs[0]), dot(tab[5], hs[1])
        for j, z in ((0, a + b), (1, a - b)):
            for m in range(2):
                for p in range(2):
                    for d in range(2):
                        at = (p, slice(m * n + j * h, m * n + (j + 1) * h), slice(d * h, (d + 1) * h))
                        lhs[at] = z[d * h : (d + 1) * h, (2 * m + p) * h : (2 * m + p + 1) * h].astype(BF16)

    def columns_back(g):
        lhs, far = lhs_s.at[g], far_s.at[g]
        a, b = dot(lhs[0], tab[2]), dot(lhs[1], tab[4])
        for j, z in ((0, a + b), (1, a - b)):
            far[j] = jnp.concatenate([z[:n], z[n:]], 1)

    def sums():
        for j in range(2):
            js = slice(j * h, (j + 1) * h)
            for m in range(2):
                s_re = s_im = None
                for g in range(GROUP):
                    g_re, g_im = far_s[g, j, :, m * n : m * n + h], far_s[g, j, :, m * n + h : (m + 1) * n]
                    o_re, o_im = win_s[g, 0, :, js], win_s[g, 1, :, js]
                    a, b = o_re * g_re + o_im * g_im, o_re * g_im - o_im * g_re
                    s_re, s_im = (a, b) if s_re is None else (s_re + a, s_im + b)
                pg_ref[2 * m, :, :, js] += s_re.reshape(shards, rows, h)
                pg_ref[2 * m + 1, :, :, js] += s_im.reshape(shards, rows, h)
            s = None
            for g in range(GROUP):
                o_re, o_im = win_s[g, 0, :, js], win_s[g, 1, :, js]
                v = o_re * o_re + o_im * o_im
                s = v if s is None else s + v
            pg_ref[4, :, :, js] += s.reshape(shards, rows, h)

    def scatter(g):
        base, fine, c = places[g]
        far = far_s.at[g]
        from_sub, from_lane = sub >= fine, lane >= c
        t = [[], []]
        for j in range(2):
            js = slice(j * h, (j + 1) * h)
            w = [None, None]
            for m in range(2):
                g_re, g_im = far[j, :, m * n : m * n + h], far[j, :, m * n + h : (m + 1) * n]
                p_re, p_im = probe_ref[m, 0, :, js], probe_ref[m, 1, :, js]
                v = (p_re * g_re + p_im * g_im, p_re * g_im - p_im * g_re)
                w = [x if y is None else x + y for x, y in zip(v, w)]
            for d in range(2):
                y = pltpu.roll(w[d].reshape(n // 8, 8, LANES), fine, 1)
                z = jnp.zeros((1, 8, LANES), F32)
                y = jnp.where(from_sub, jnp.concatenate([y, z], 0), jnp.concatenate([z, y], 0))
                t[d].append(pltpu.roll(y, c, 2))
        for d in range(2):
            a, b = t[d]
            out = [jnp.where(from_lane, a, 0.0), jnp.where(from_lane, b, a), jnp.where(from_lane, 0.0, b)]
            for q in range(3):
                grad[d, pl.ds(base + below_row, n + 8), LANES * q : LANES * (q + 1)] += out[q].reshape(n + 8, LANES)

    for stage in (load, wave, columns, down, weigh, up, columns_back):
        for g in range(GROUP):
            stage(g)
    sums()
    for g in range(GROUP):
        scatter(g)

    @pl.when(k == pl.num_programs(0) - 1)
    def _():
        if first:
            out = [(grad, grad_out), (pg_ref, pg_out), (loss_ref, loss_out)]
            out = [pltpu.make_async_copy(a, b, sems.at[i]) for i, (a, b) in enumerate(out)]
            for copy in out:
                copy.start()
            for copy in out:
                copy.wait()
            return
        out = [(grad.at[:, pl.ds(2 * n, n)], low_out), (grad.at[:, pl.ds(0, 2 * n)], grad_out), (away_ref, away_out), (keep_ref, keep_out)]
        out = [pltpu.make_async_copy(a, b, sems.at[i]) for i, (a, b) in enumerate(out)]
        out[0].start()
        out[1].start()
        me = off_ref[off_ref.shape[0] - 1, 0]
        loss = loss_ref[:, : n // 2] + loss_ref[:, n // 2 :]
        for core in (1, 0):
            ref = away_ref if core else keep_ref
            for slot in range(shards // 2):
                owner = owner_of(me, core, slot, shards)
                for q in range(5):
                    value = pg_ref[q, owner]
                    ref[slot, 2 * q * rows : (2 * q + 1) * rows] = value[:, : n // 2]
                    ref[slot, (2 * q + 1) * rows : (2 * q + 2) * rows] = value[:, n // 2 :]
                ref[slot, 10 * rows :] = loss
            out[3 - core].start()
        for copy in out:
            copy.wait()


def owner_of(me, core, slot, size):
    z = lax.rem(me // 4 + slot % (size // 4), size // 4)
    return z * 4 + ((me & 3) ^ (core + 2 * (slot // (size // 4))))


def windows(first, shards, count, offs, object_field, probe, amplitude, amp_first, table, carried=()):
    n = probe.shape[-1]
    width = object_field.shape[2]
    sums = (5, shards, n // shards, n)
    hbm, anywhere = pl.BlockSpec(memory_space=pltpu.HBM), pl.BlockSpec(memory_space=pl.ANY)
    inputs = (object_field, probe, amplitude, table, *carried)
    scratch = []
    if first:
        shapes = [(2, 2 * n, width), sums, (8, n)]
    else:
        slots = (shards // 2, 10 * (n // shards) + 8, n // 2)
        shapes = [(2, 2 * n, width), (2, n, width), slots, slots]
        scratch += [pltpu.VMEM(slots, F32)] * 2
    scratch += [
        pltpu.VMEM((2, 2 * n, width), F32),
        pltpu.VMEM((2, 2 * n if first else 3 * n, width), F32),
        pltpu.VMEM(sums, F32),
        pltpu.VMEM((8, n), F32),
        pltpu.VMEM(probe.shape, F32),
        pltpu.VMEM(table.shape, BF16),
        pltpu.VMEM((count // GROUP, 2, GROUP, n, LANES), F32),
        pltpu.VMEM((GROUP, 2, n, n), F32),
        pltpu.VMEM((GROUP, 2, 2 * n, n), BF16),
        pltpu.VMEM((GROUP, 2, n, 2 * n), BF16),
        pltpu.VMEM((GROUP, 2, n, 2 * n), F32),
        pltpu.SemaphoreType.DMA((12,)),
    ]
    return pl.pallas_call(
        functools.partial(windows_kernel, first, amp_first),
        grid_spec=pltpu.PrefetchScalarGridSpec(
            num_scalar_prefetch=1,
            grid=(count // GROUP,),
            in_specs=[anywhere] * len(inputs),
            out_specs=[anywhere] * len(shapes),
            scratch_shapes=scratch,
        ),
        out_shape=[jax.ShapeDtypeStruct(s, F32) for s in shapes],
        compiler_params=pltpu.CompilerParams(vmem_limit_bytes=(48 if first else 20) << 20),
        name="near" if first else "across",
    )(offs, *inputs)


def place_kernel(nears, scale, me_ref, *refs):
    pieces, refs = refs[: len(nears)], refs[len(nears) :]
    if scale:
        losses_ref, out_ref, loss_ref, stage, sem = refs
    else:
        unused, out_ref, stage, sem = refs
    quarter, planes, rows, n = pieces[0].shape
    me = me_ref[0]
    copies = [pltpu.make_async_copy(piece, stage.at[i], sem.at[i, quarter]) for i, piece in enumerate(pieces)]
    for copy in copies:
        copy.start()
    if scale:
        loss = jnp.zeros(losses_ref.shape[1:], F32)
        for z in range(quarter):
            loss = loss + losses_ref[lax.rem(me // 4 + quarter - z, quarter)]
        loss_ref[0] = jnp.sum(loss) * scale
    out = []
    for i, near in enumerate(nears):
        copies[i].wait()
        for z in range(quarter):
            owner = owner_of(me, near, z, 4 * quarter)
            out.append(pltpu.make_async_copy(stage.at[i, z], out_ref.at[:, owner], sem.at[i, z]))
            out[-1].start()
    for copy in out:
        copy.wait()


def place(me, nears, pieces, losses=None, scale=None, base=None):
    quarter, planes, rows, n = pieces[0].shape
    shape = (planes, 4 * quarter, rows, n)
    anywhere, hbm = pl.BlockSpec(memory_space=pl.ANY), pl.BlockSpec(memory_space=pltpu.HBM)
    smem = pl.BlockSpec(memory_space=pltpu.SMEM)
    in_specs = [smem] + [anywhere] * len(pieces)
    out_specs, out_shape, aliases = [hbm], [jax.ShapeDtypeStruct(shape, F32)], {}
    if scale:
        in_specs, last = in_specs + [pl.BlockSpec(memory_space=pltpu.VMEM)], losses
        out_specs, out_shape = out_specs + [smem], out_shape + [jax.ShapeDtypeStruct((1,), F32)]
    else:
        in_specs, last = in_specs + [hbm], base
        aliases = {1 + len(pieces): 0}
    return pl.pallas_call(
        functools.partial(place_kernel, nears, scale),
        in_specs=in_specs,
        out_specs=out_specs,
        out_shape=out_shape,
        scratch_shapes=[
            pltpu.VMEM((len(nears), *pieces[0].shape), F32),
            pltpu.SemaphoreType.DMA((len(nears), quarter + 1)),
        ],
        input_output_aliases=aliases,
        compiler_params=pltpu.CompilerParams(vmem_limit_bytes=4 << 20),
        name="place",
    )(me.reshape(1), *pieces, last)


def swap(x, bit):
    size = lax.axis_size("row")
    return lax.ppermute(x, "row", [(i, i ^ bit) for i in range(size)])


def shift(x, by):
    size = lax.axis_size("row")
    return lax.ppermute(x, "row", [(i, (i + by) % size) for i in range(size)])


def tree(parts):
    while len(parts) > 1:
        parts = [sum(parts[i + 1 : i + 2], parts[i]) for i in range(0, len(parts), 2)]
    return parts[0]


def per_device(object_field, probe, amplitude, offsets):
    tile = object_field.shape[1]
    n = probe.shape[2]
    count = offsets.shape[0]
    near = count // 2
    size = lax.axis_size("row")
    me = lax.axis_index("row")
    table = jnp.asarray(dft_tables(n))
    below = lax.ppermute(object_field[:, :n], "row", [(i, i - 1) for i in range(1, size)])
    offs = jnp.concatenate([offsets - jnp.stack([me * tile, 0]), jnp.stack([me, 0])[None]])
    grad, pg, loss = windows(True, size, near, offs, object_field, probe, amplitude, 0, table)
    grad, low, keep, away = windows(
        False, size, count - near, offs, object_field, probe, amplitude, near, table, (below, grad, pg, loss)
    )
    hop = lax.ppermute(low, "row", [(i, i + 4) for i in range(3, size - 4, 4)])
    rows = n // size
    quarter = size // 4
    away = swap(away, 1)
    beside = swap(keep[quarter:] + away[quarter:], 2)
    x = keep[:quarter] + away[:quarter] + beside
    hop, x = lax.optimization_barrier((hop, x))
    carried = jnp.where(me % 4 == 3, hop, low)
    carried = lax.ppermute(carried, "row", [(i, i - 3 if i % 4 == 3 else i + 1) for i in range(size)])
    parts = [x[0]] + [shift(x[z], 4 * z) for z in range(1, quarter)]
    total = tree(parts)
    losses = jnp.stack([p[10 * rows :] for p in parts])
    planes = total[: 10 * rows].reshape(5, 2, rows, n // 2)
    y = planes[:4] / jnp.sqrt(planes[4] + 1.0)
    y = jnp.concatenate([y[:, 0], y[:, 1]], -1)
    y = jnp.stack([y] + [shift(y, -4 * z) for z in range(1, quarter)])
    sibling = swap(y, 1)
    beside = swap(y, 2)
    probe_dir, loss = place(me, (0, 1), (y, sibling), losses, 1.0 / (count * size * n * n))
    object_grad = grad.at[:, :n].add(carried)
    probe_dir, object_grad, beside = lax.optimization_barrier((probe_dir, object_grad, beside))
    sibling = swap(beside, 1)
    (probe_dir,) = place(me, (2,), (beside,), base=probe_dir)
    (probe_dir,) = place(me, (3,), (sibling,), base=probe_dir)
    probe_dir = probe_dir.reshape(2, 2, n, n)
    return (object_grad, probe_dir, loss)


def solution(mesh):
    placed = (
        P(None, ("groups", "row"), None),
        P(),
        P(("groups", "row"), None, None),
        P(("groups", "row"), None),
    )
    return jax.shard_map(
        per_device,
        mesh=mesh,
        in_specs=placed,
        out_specs=(P(None, ("groups", "row"), None), P("groups", None, None, None), P("groups")),
        check_vma=False,
    )
```

```python
import functools
import math

import jax
import jax.numpy as jnp
import ml_dtypes
import numpy as np
from jax import lax
from jax.experimental import pallas as pl
from jax.experimental.pallas import tpu as pltpu
from jax.sharding import PartitionSpec as P

F32, BF16 = jnp.float32, jnp.bfloat16
LANES = 128
GROUP = 2
VMEM_MIB = 30


def dft_tables(n):
    h = n // 2
    idx = np.arange(n)
    angle = (idx[:, None] * idx[None, :] % n).astype(np.float32) * np.float32(2.0 * math.pi / n)
    scale = np.float32(1.0 / math.sqrt(n))
    c, s = np.cos(angle) * scale, np.sin(angle) * scale
    near = np.arange(h)
    even, odd = 2 * near, 2 * near + 1
    turned = 2 * ((near + h // 2) % h) + 1

    def column(k):
        a, b = c[np.ix_(near, k)], s[np.ix_(near, k)]
        return np.block([[a, -b], [b, a]])

    def row(r):
        a, b = c[np.ix_(r, near)], s[np.ix_(r, near)]
        return np.block([[a, b], [-b, a]])

    tables = [column(even), column(turned), row(even), row(odd)]
    return np.stack(tables + [tables[1].T, tables[3].T]).astype(ml_dtypes.bfloat16)


def windows_kernel(first, amp_first, off_ref, *refs):
    object_ref, probe_hbm, amp_hbm, tab_hbm = refs[:4]
    if first:
        grad_out, pg_out, loss_out = refs[4:7]
    else:
        below_ref, grad_in, pg_in, loss_in, grad_out, low_out, keep_out, away_out, keep_ref, away_ref = refs[4:14]
    ext, grad, pg_ref, loss_ref, probe_ref, tab, amp_s, win_s, lhs_s, hs_s, far_s, sems = refs[-12:]
    shards, rows = pg_ref.shape[1:3]
    k = pl.program_id(0)
    n = probe_ref.shape[-1]
    h = n // 2
    width = ext.shape[2]
    below_row = 0 if first else n
    lane = lax.broadcasted_iota(jnp.int32, (1, 1, LANES), 2)
    sub = lax.broadcasted_iota(jnp.int32, (1, 8, 1), 1)

    def amplitude_copies(group):
        at = amp_first + group * GROUP
        return [
            pltpu.make_async_copy(
                amp_hbm.at[pl.ds(at, GROUP), :, pl.ds(q * LANES, LANES)], amp_s.at[group, q], sems.at[8 + 2 * group + q]
            )
            for q in range(2)
        ]

    if first:
        windows_in = [(object_ref, ext)]
        sums_in = []
    else:
        windows_in = [(object_ref.at[:, pl.ds(n, n)], ext.at[:, pl.ds(0, n)]), (below_ref, ext.at[:, pl.ds(n, n)])]
        sums_in = [(grad_in, grad.at[:, pl.ds(0, 2 * n)]), (pg_in, pg_ref), (loss_in, loss_ref)]
    windows_in = [*windows_in, (probe_hbm, probe_ref)]
    windows_in = [pltpu.make_async_copy(a, b, sems.at[i]) for i, (a, b) in enumerate(windows_in)]
    table_in = pltpu.make_async_copy(tab_hbm, tab, sems.at[3])
    sums_in = [pltpu.make_async_copy(a, b, sems.at[4 + i]) for i, (a, b) in enumerate(sums_in)]

    @pl.when(k == 0)
    def _():
        for copy in (*windows_in, table_in, *amplitude_copies(0), *amplitude_copies(1), *sums_in):
            copy.start()
        if first:
            grad[...] = jnp.zeros_like(grad)
            pg_ref[...] = jnp.zeros_like(pg_ref)
            loss_ref[...] = jnp.zeros_like(loss_ref)
        else:
            grad[:, 2 * n :] = jnp.zeros((2, n, width), F32)
        for copy in (*windows_in, table_in, *sums_in):
            copy.wait()

    for copy in amplitude_copies(k):
        copy.wait()

    def dot(a, b):
        return jnp.dot(a, b, preferred_element_type=F32)

    places = []
    for g in range(GROUP):
        r, c = off_ref[amp_first + k * GROUP + g, 0] - below_row, off_ref[amp_first + k * GROUP + g, 1]
        fine = lax.rem(r, 8)
        places.append((pl.multiple_of(r - fine, 8), fine, c))

    def load(g):
        base, fine, c = places[g]
        win = win_s.at[g]
        in_lane, in_sub = lane < LANES - c, sub < 8 - fine
        back_lane, back_sub = lax.rem(LANES - c, LANES), lax.rem(8 - fine, 8)
        for d in range(2):
            x = ext[d, pl.ds(base, n + 8), :].reshape(n // 8 + 1, 8, width)
            t = [pltpu.roll(x[:, :, LANES * q : LANES * (q + 1)], back_lane, 2) for q in range(3)]
            for q in range(2):
                y = pltpu.roll(jnp.where(in_lane, t[q], t[q + 1]), back_sub, 1)
                win[d, :, LANES * q : LANES * (q + 1)] = jnp.where(in_sub, y[:-1], y[1:]).reshape(n, LANES)

    def wave(g):
        win, lhs = win_s.at[g], lhs_s.at[g]
        for m in range(2):
            parts = []
            for j in range(2):
                js = slice(j * h, (j + 1) * h)
                p_re, p_im = probe_ref[m, 0, :, js], probe_ref[m, 1, :, js]
                o_re, o_im = win[0, :, js], win[1, :, js]
                parts.append((p_re * o_re - p_im * o_im, p_re * o_im + p_im * o_re))
            for d in range(2):
                at = (slice(m * n, (m + 1) * n), slice(d * h, (d + 1) * h))
                lhs[(0, *at)] = (parts[0][d] + parts[1][d]).astype(BF16)
                lhs[(1, *at)] = (parts[0][d] - parts[1][d]).astype(BF16)

    def columns(g):
        lhs, hs = lhs_s.at[g], hs_s.at[g]
        for p in range(2):
            v = dot(lhs[p], tab[p])
            for m in range(2):
                top, bottom = v[m * n : m * n + h], v[m * n + h : (m + 1) * n]
                for u, z in ((0, top + bottom), (1, top - bottom)):
                    for d in range(2):
                        at = (u, slice(d * h, (d + 1) * h), slice((2 * m + p) * h, (2 * m + p + 1) * h))
                        hs[at] = z[:, d * h : (d + 1) * h].astype(BF16)

    def down(g):
        hs, far = hs_s.at[g], far_s.at[g]
        for u in range(2):
            far[u] = dot(tab[2 + u], hs[u])

    idx = lax.broadcasted_iota(jnp.int32, (h, LANES), 1)
    lower = idx < LANES // 2
    pick_lo = jnp.where(lower, 2 * idx, 2 * idx - (LANES - 1))
    pick_hi = jnp.where(lower, 2 * idx + 1, 2 * idx - LANES)

    def weigh(g):
        hs, far = hs_s.at[g], far_s.at[g]
        total = jnp.zeros((8, n), F32)
        for u in range(2):
            lo = jnp.take_along_axis(amp_s[k, 0, g, pl.ds(u, h, stride=2), :], pick_lo, 1)
            hi = jnp.take_along_axis(amp_s[k, 1, g, pl.ds(u, h, stride=2), :], pick_hi, 1)
            amplitude = jnp.concatenate([jnp.where(lower, lo, hi), jnp.where(lower, hi, lo)], 1)
            power = None
            for e in range(2):
                for m in range(2):
                    f = far[u, e * h : (e + 1) * h, m * n : (m + 1) * n]
                    power = f * f if power is None else power + f * f
            magnitude = jnp.sqrt(power)
            miss = magnitude - amplitude
            total = total + jnp.sum((miss * miss).reshape(h // 8, 8, n), 0)
            weight = 0.25 * (1.0 - amplitude / jnp.maximum(magnitude, 0.5))
            for e in range(2):
                for m in range(2):
                    at = (u, slice(e * h, (e + 1) * h), slice(m * n, (m + 1) * n))
                    hs[at] = (weight * far[at]).astype(BF16)
        loss_ref[...] += total

    def up(g):
        lhs, hs = lhs_s.at[g], hs_s.at[g]
        a, b = dot(tab[0], hs[0]), dot(tab[5], hs[1])
        for j, z in ((0, a + b), (1, a - b)):
            for m in range(2):
                for p in range(2):
                    for d in range(2):
                        at = (p, slice(m * n + j * h, m * n + (j + 1) * h), slice(d * h, (d + 1) * h))
                        lhs[at] = z[d * h : (d + 1) * h, (2 * m + p) * h : (2 * m + p + 1) * h].astype(BF16)

    def columns_back(g):
        lhs, far = lhs_s.at[g], far_s.at[g]
        a, b = dot(lhs[0], tab[2]), dot(lhs[1], tab[4])
        for j, z in ((0, a + b), (1, a - b)):
            far[j] = jnp.concatenate([z[:n], z[n:]], 1)

    def sums():
        for j in range(2):
            js = slice(j * h, (j + 1) * h)
            for m in range(2):
                s_re = s_im = None
                for g in range(GROUP):
                    g_re, g_im = far_s[g, j, :, m * n : m * n + h], far_s[g, j, :, m * n + h : (m + 1) * n]
                    o_re, o_im = win_s[g, 0, :, js], win_s[g, 1, :, js]
                    a, b = o_re * g_re + o_im * g_im, o_re * g_im - o_im * g_re
                    s_re, s_im = (a, b) if s_re is None else (s_re + a, s_im + b)
                pg_ref[2 * m, :, :, js] += s_re.reshape(shards, rows, h)
                pg_ref[2 * m + 1, :, :, js] += s_im.reshape(shards, rows, h)
            s = None
            for g in range(GROUP):
                o_re, o_im = win_s[g, 0, :, js], win_s[g, 1, :, js]
                v = o_re * o_re + o_im * o_im
                s = v if s is None else s + v
            pg_ref[4, :, :, js] += s.reshape(shards, rows, h)

    def scatter(g):
        base, fine, c = places[g]
        far = far_s.at[g]
        from_sub, from_lane = sub >= fine, lane >= c
        t = [[], []]
        for j in range(2):
            js = slice(j * h, (j + 1) * h)
            w = [None, None]
            for m in range(2):
                g_re, g_im = far[j, :, m * n : m * n + h], far[j, :, m * n + h : (m + 1) * n]
                p_re, p_im = probe_ref[m, 0, :, js], probe_ref[m, 1, :, js]
                v = (p_re * g_re + p_im * g_im, p_re * g_im - p_im * g_re)
                w = [x if y is None else x + y for x, y in zip(v, w)]
            for d in range(2):
                y = pltpu.roll(w[d].reshape(n // 8, 8, LANES), fine, 1)
                z = jnp.zeros((1, 8, LANES), F32)
                y = jnp.where(from_sub, jnp.concatenate([y, z], 0), jnp.concatenate([z, y], 0))
                t[d].append(pltpu.roll(y, c, 2))
        for d in range(2):
            a, b = t[d]
            out = [jnp.where(from_lane, a, 0.0), jnp.where(from_lane, b, a), jnp.where(from_lane, 0.0, b)]
            for q in range(3):
                grad[d, pl.ds(base + below_row, n + 8), LANES * q : LANES * (q + 1)] += out[q].reshape(n + 8, LANES)

    for stage in (load, wave, columns, down, weigh, up, columns_back):
        for g in range(GROUP):
            stage(g)
    sums()
    for g in range(GROUP):
        scatter(g)

    @pl.when(k == pl.num_programs(0) - 1)
    def _():
        if first:
            out = [(grad, grad_out), (pg_ref, pg_out), (loss_ref, loss_out)]
            out = [pltpu.make_async_copy(a, b, sems.at[i]) for i, (a, b) in enumerate(out)]
            for copy in out:
                copy.start()
            for copy in out:
                copy.wait()
            return
        out = [(grad.at[:, pl.ds(2 * n, n)], low_out), (grad.at[:, pl.ds(0, 2 * n)], grad_out), (away_ref, away_out), (keep_ref, keep_out)]
        out = [pltpu.make_async_copy(a, b, sems.at[i]) for i, (a, b) in enumerate(out)]
        out[0].start()
        out[1].start()
        me = off_ref[off_ref.shape[0] - 1, 0]
        loss = loss_ref[:, : n // 2] + loss_ref[:, n // 2 :]
        for core in (1, 0):
            ref = away_ref if core else keep_ref
            for slot in range(shards // 2):
                owner = owner_of(me, core, slot, shards)
                for q in range(5):
                    value = pg_ref[q, owner]
                    ref[slot, 2 * q * rows : (2 * q + 1) * rows] = value[:, : n // 2]
                    ref[slot, (2 * q + 1) * rows : (2 * q + 2) * rows] = value[:, n // 2 :]
                ref[slot, 10 * rows :] = loss
            out[3 - core].start()
        for copy in out:
            copy.wait()


def owner_of(me, core, slot, size):
    z = lax.rem(me // 4 + slot % (size // 4), size // 4)
    return z * 4 + ((me & 3) ^ (core + 2 * (slot // (size // 4))))


def windows(first, shards, count, offs, object_field, probe, amplitude, amp_first, table, carried=()):
    n = probe.shape[-1]
    width = object_field.shape[2]
    sums = (5, shards, n // shards, n)
    hbm, anywhere = pl.BlockSpec(memory_space=pltpu.HBM), pl.BlockSpec(memory_space=pl.ANY)
    inputs = (object_field, probe, amplitude, table, *carried)
    scratch = []
    if first:
        shapes = [(2, 2 * n, width), sums, (8, n)]
    else:
        slots = (shards // 2, 10 * (n // shards) + 8, n // 2)
        shapes = [(2, 2 * n, width), (2, n, width), slots, slots]
        scratch += [pltpu.VMEM(slots, F32)] * 2
    scratch += [
        pltpu.VMEM((2, 2 * n, width), F32),
        pltpu.VMEM((2, 2 * n if first else 3 * n, width), F32),
        pltpu.VMEM(sums, F32),
        pltpu.VMEM((8, n), F32),
        pltpu.VMEM(probe.shape, F32),
        pltpu.VMEM(table.shape, BF16),
        pltpu.VMEM((count // GROUP, 2, GROUP, n, LANES), F32),
        pltpu.VMEM((GROUP, 2, n, n), F32),
        pltpu.VMEM((GROUP, 2, 2 * n, n), BF16),
        pltpu.VMEM((GROUP, 2, n, 2 * n), BF16),
        pltpu.VMEM((GROUP, 2, n, 2 * n), F32),
        pltpu.SemaphoreType.DMA((12,)),
    ]
    return pl.pallas_call(
        functools.partial(windows_kernel, first, amp_first),
        grid_spec=pltpu.PrefetchScalarGridSpec(
            num_scalar_prefetch=1,
            grid=(count // GROUP,),
            in_specs=[anywhere] * len(inputs),
            out_specs=[anywhere] * len(shapes),
            scratch_shapes=scratch,
        ),
        out_shape=[jax.ShapeDtypeStruct(s, F32) for s in shapes],
        compiler_params=pltpu.CompilerParams(vmem_limit_bytes=(48 if first else 20) << 20),
        name="near" if first else "across",
    )(offs, *inputs)


def place_kernel(nears, scale, me_ref, *refs):
    pieces, refs = refs[: len(nears)], refs[len(nears) :]
    if scale:
        losses_ref, out_ref, loss_ref, stage, sem = refs
    else:
        unused, out_ref, stage, sem = refs
    quarter, planes, rows, n = pieces[0].shape
    me = me_ref[0]
    copies = [pltpu.make_async_copy(piece, stage.at[i], sem.at[i, quarter]) for i, piece in enumerate(pieces)]
    for copy in copies:
        copy.start()
    if scale:
        loss = jnp.zeros(losses_ref.shape[1:], F32)
        for z in range(quarter):
            loss = loss + losses_ref[lax.rem(me // 4 + quarter - z, quarter)]
        loss_ref[0] = jnp.sum(loss) * scale
    out = []
    for i, near in enumerate(nears):
        copies[i].wait()
        for z in range(quarter):
            owner = owner_of(me, near, z, 4 * quarter)
            out.append(pltpu.make_async_copy(stage.at[i, z], out_ref.at[:, owner], sem.at[i, z]))
            out[-1].start()
    for copy in out:
        copy.wait()


def place(me, nears, pieces, losses=None, scale=None, base=None):
    quarter, planes, rows, n = pieces[0].shape
    shape = (planes, 4 * quarter, rows, n)
    anywhere, hbm = pl.BlockSpec(memory_space=pl.ANY), pl.BlockSpec(memory_space=pltpu.HBM)
    smem = pl.BlockSpec(memory_space=pltpu.SMEM)
    in_specs = [smem] + [anywhere] * len(pieces)
    out_specs, out_shape, aliases = [hbm], [jax.ShapeDtypeStruct(shape, F32)], {}
    if scale:
        in_specs, last = in_specs + [pl.BlockSpec(memory_space=pltpu.VMEM)], losses
        out_specs, out_shape = out_specs + [smem], out_shape + [jax.ShapeDtypeStruct((1,), F32)]
    else:
        in_specs, last = in_specs + [hbm], base
        aliases = {1 + len(pieces): 0}
    return pl.pallas_call(
        functools.partial(place_kernel, nears, scale),
        in_specs=in_specs,
        out_specs=out_specs,
        out_shape=out_shape,
        scratch_shapes=[
            pltpu.VMEM((len(nears), *pieces[0].shape), F32),
            pltpu.SemaphoreType.DMA((len(nears), quarter + 1)),
        ],
        input_output_aliases=aliases,
        compiler_params=pltpu.CompilerParams(vmem_limit_bytes=4 << 20),
        name="place",
    )(me.reshape(1), *pieces, last)


def swap(x, bit):
    size = lax.axis_size("row")
    return lax.ppermute(x, "row", [(i, i ^ bit) for i in range(size)])


def shift(x, by):
    size = lax.axis_size("row")
    return lax.ppermute(x, "row", [(i, (i + by) % size) for i in range(size)])


def tree(parts):
    while len(parts) > 1:
        parts = [sum(parts[i + 1 : i + 2], parts[i]) for i in range(0, len(parts), 2)]
    return parts[0]


def per_device(object_field, probe, amplitude, offsets):
    tile = object_field.shape[1]
    n = probe.shape[2]
    count = offsets.shape[0]
    near = count // 2
    size = lax.axis_size("row")
    me = lax.axis_index("row")
    table = jnp.asarray(dft_tables(n))
    below = lax.ppermute(object_field[:, :n], "row", [(i, i - 1) for i in range(1, size)])
    offs = jnp.concatenate([offsets - jnp.stack([me * tile, 0]), jnp.stack([me, 0])[None]])
    grad, pg, loss = windows(True, size, near, offs, object_field, probe, amplitude, 0, table)
    grad, low, keep, away = windows(
        False, size, count - near, offs, object_field, probe, amplitude, near, table, (below, grad, pg, loss)
    )
    hop = lax.ppermute(low, "row", [(i, i + 4) for i in range(3, size - 4, 4)])
    rows = n // size
    quarter = size // 4
    away = swap(away, 1)
    beside = swap(keep[quarter + 1 :] + away[quarter + 1 :], 2)
    x = keep[1:quarter] + away[1:quarter] + beside
    hop, x = lax.optimization_barrier((hop, x))
    own = keep[0] + away[0] + swap(keep[quarter] + away[quarter], 2)
    carried = jnp.where(me % 4 == 3, hop, low)
    carried = lax.ppermute(carried, "row", [(i, i - 3 if i % 4 == 3 else i + 1) for i in range(size)])
    parts = [own] + [shift(x[z - 1], 4 * z) for z in range(1, quarter)]
    total = tree(parts)
    losses = jnp.stack([p[10 * rows :] for p in parts])
    planes = total[: 10 * rows].reshape(5, 2, rows, n // 2)
    y = planes[:4] / jnp.sqrt(planes[4] + 1.0)
    y = jnp.concatenate([y[:, 0], y[:, 1]], -1)
    others = jnp.stack([shift(y, -4 * z) for z in range(1, quarter)])
    first = swap(y, 2)
    y = jnp.concatenate([y[None], others])
    sibling = swap(y, 1)
    beside = jnp.concatenate([first[None], swap(others, 2)])
    probe_dir, loss = place(me, (0,), (y,), losses, 1.0 / (count * size * n * n))
    object_grad = grad.at[:, :n].add(carried)
    probe_dir, object_grad, beside = lax.optimization_barrier((probe_dir, object_grad, beside))
    farther = swap(beside, 1)
    (probe_dir,) = place(me, (1, 2), (sibling, beside), base=probe_dir)
    (probe_dir,) = place(me, (3,), (farther,), base=probe_dir)
    probe_dir = probe_dir.reshape(2, 2, n, n)
    return (object_grad, probe_dir, loss)


def solution(mesh):
    placed = (
        P(None, ("groups", "row"), None),
        P(),
        P(("groups", "row"), None, None),
        P(("groups", "row"), None),
    )
    return jax.shard_map(
        per_device,
        mesh=mesh,
        in_specs=placed,
        out_specs=(P(None, ("groups", "row"), None), P("groups", None, None, None), P("groups")),
        check_vma=False,
    )
```

```python
import functools
import math

import jax
import jax.numpy as jnp
import ml_dtypes
import numpy as np
from jax import lax
from jax.experimental import pallas as pl
from jax.experimental.pallas import tpu as pltpu
from jax.sharding import PartitionSpec as P

F32, BF16 = jnp.float32, jnp.bfloat16
LANES = 128
GROUP = 2
VMEM_MIB = 30


def dft_tables(n):
    h = n // 2
    idx = np.arange(n)
    angle = (idx[:, None] * idx[None, :] % n).astype(np.float32) * np.float32(2.0 * math.pi / n)
    scale = np.float32(1.0 / math.sqrt(n))
    c, s = np.cos(angle) * scale, np.sin(angle) * scale
    near = np.arange(h)
    even, odd = 2 * near, 2 * near + 1
    turned = 2 * ((near + h // 2) % h) + 1

    def column(k):
        a, b = c[np.ix_(near, k)], s[np.ix_(near, k)]
        return np.block([[a, -b], [b, a]])

    def row(r):
        a, b = c[np.ix_(r, near)], s[np.ix_(r, near)]
        return np.block([[a, b], [-b, a]])

    tables = [column(even), column(turned), row(even), row(odd)]
    return np.stack(tables + [tables[1].T, tables[3].T]).astype(ml_dtypes.bfloat16)


def windows_kernel(first, amp_first, group_size, off_ref, *refs):
    object_ref, probe_hbm, amp_hbm, tab_hbm = refs[:4]
    if first:
        grad_out, pg_out, loss_out = refs[4:7]
    else:
        below_ref, grad_in, pg_in, loss_in, grad_out, low_out, keep_out, away_out, keep_ref, away_ref = refs[4:14]
    ext, grad, pg_ref, loss_ref, probe_ref, tab, amp_s, win_s, lhs_s, hs_s, far_s, sems = refs[-12:]
    shards, rows = pg_ref.shape[1:3]
    k = pl.program_id(0)
    n = probe_ref.shape[-1]
    h = n // 2
    width = ext.shape[2]
    below_row = 0 if first else n
    lane = lax.broadcasted_iota(jnp.int32, (1, 1, LANES), 2)
    sub = lax.broadcasted_iota(jnp.int32, (1, 8, 1), 1)

    def amplitude_copies(group):
        at = amp_first + group * group_size
        return [
            pltpu.make_async_copy(
                amp_hbm.at[pl.ds(at, group_size), :, pl.ds(q * LANES, LANES)], amp_s.at[group, q], sems.at[8 + 2 * group + q]
            )
            for q in range(2)
        ]

    if first:
        windows_in = [(object_ref, ext)]
        sums_in = []
    else:
        windows_in = [(object_ref.at[:, pl.ds(n, n)], ext.at[:, pl.ds(0, n)]), (below_ref, ext.at[:, pl.ds(n, n)])]
        sums_in = [(grad_in, grad.at[:, pl.ds(0, 2 * n)]), (pg_in, pg_ref), (loss_in, loss_ref)]
    windows_in = [*windows_in, (probe_hbm, probe_ref)]
    windows_in = [pltpu.make_async_copy(a, b, sems.at[i]) for i, (a, b) in enumerate(windows_in)]
    table_in = pltpu.make_async_copy(tab_hbm, tab, sems.at[3])
    sums_in = [pltpu.make_async_copy(a, b, sems.at[4 + i]) for i, (a, b) in enumerate(sums_in)]

    @pl.when(k == 0)
    def _():
        for copy in (*windows_in, table_in, *[c for i in range(amp_s.shape[0]) for c in amplitude_copies(i)], *sums_in):
            copy.start()
        if first:
            grad[...] = jnp.zeros_like(grad)
            pg_ref[...] = jnp.zeros_like(pg_ref)
            loss_ref[...] = jnp.zeros_like(loss_ref)
        else:
            grad[:, 2 * n :] = jnp.zeros((2, n, width), F32)
        for copy in (*windows_in, table_in, *sums_in):
            copy.wait()

    for copy in amplitude_copies(k):
        copy.wait()

    def dot(a, b):
        return jnp.dot(a, b, preferred_element_type=F32)

    places = []
    for g in range(group_size):
        r, c = off_ref[amp_first + k * group_size + g, 0] - below_row, off_ref[amp_first + k * group_size + g, 1]
        fine = lax.rem(r, 8)
        places.append((pl.multiple_of(r - fine, 8), fine, c))

    def load(g):
        base, fine, c = places[g]
        win = win_s.at[g]
        in_lane, in_sub = lane < LANES - c, sub < 8 - fine
        back_lane, back_sub = lax.rem(LANES - c, LANES), lax.rem(8 - fine, 8)
        for d in range(2):
            x = ext[d, pl.ds(base, n + 8), :].reshape(n // 8 + 1, 8, width)
            t = [pltpu.roll(x[:, :, LANES * q : LANES * (q + 1)], back_lane, 2) for q in range(3)]
            for q in range(2):
                y = pltpu.roll(jnp.where(in_lane, t[q], t[q + 1]), back_sub, 1)
                win[d, :, LANES * q : LANES * (q + 1)] = jnp.where(in_sub, y[:-1], y[1:]).reshape(n, LANES)

    def wave(g):
        win, lhs = win_s.at[g], lhs_s.at[g]
        for m in range(2):
            parts = []
            for j in range(2):
                js = slice(j * h, (j + 1) * h)
                p_re, p_im = probe_ref[m, 0, :, js], probe_ref[m, 1, :, js]
                o_re, o_im = win[0, :, js], win[1, :, js]
                parts.append((p_re * o_re - p_im * o_im, p_re * o_im + p_im * o_re))
            for d in range(2):
                at = (slice(m * n, (m + 1) * n), slice(d * h, (d + 1) * h))
                lhs[(0, *at)] = (parts[0][d] + parts[1][d]).astype(BF16)
                lhs[(1, *at)] = (parts[0][d] - parts[1][d]).astype(BF16)

    def columns(g):
        lhs, hs = lhs_s.at[g], hs_s.at[g]
        for p in range(2):
            v = dot(lhs[p], tab[p])
            for m in range(2):
                top, bottom = v[m * n : m * n + h], v[m * n + h : (m + 1) * n]
                for u, z in ((0, top + bottom), (1, top - bottom)):
                    for d in range(2):
                        at = (u, slice(d * h, (d + 1) * h), slice((2 * m + p) * h, (2 * m + p + 1) * h))
                        hs[at] = z[:, d * h : (d + 1) * h].astype(BF16)

    def down(g):
        hs, far = hs_s.at[g], far_s.at[g]
        for u in range(2):
            far[u] = dot(tab[2 + u], hs[u])

    idx = lax.broadcasted_iota(jnp.int32, (h, LANES), 1)
    lower = idx < LANES // 2
    pick_lo = jnp.where(lower, 2 * idx, 2 * idx - (LANES - 1))
    pick_hi = jnp.where(lower, 2 * idx + 1, 2 * idx - LANES)

    def weigh(g):
        hs, far = hs_s.at[g], far_s.at[g]
        total = jnp.zeros((8, n), F32)
        for u in range(2):
            lo = jnp.take_along_axis(amp_s[k, 0, g, pl.ds(u, h, stride=2), :], pick_lo, 1)
            hi = jnp.take_along_axis(amp_s[k, 1, g, pl.ds(u, h, stride=2), :], pick_hi, 1)
            amplitude = jnp.concatenate([jnp.where(lower, lo, hi), jnp.where(lower, hi, lo)], 1)
            power = None
            for e in range(2):
                for m in range(2):
                    f = far[u, e * h : (e + 1) * h, m * n : (m + 1) * n]
                    power = f * f if power is None else power + f * f
            magnitude = jnp.sqrt(power)
            miss = magnitude - amplitude
            total = total + jnp.sum((miss * miss).reshape(h // 8, 8, n), 0)
            weight = 0.25 * (1.0 - amplitude / jnp.maximum(magnitude, 0.5))
            for e in range(2):
                for m in range(2):
                    at = (u, slice(e * h, (e + 1) * h), slice(m * n, (m + 1) * n))
                    hs[at] = (weight * far[at]).astype(BF16)
        loss_ref[...] += total

    def up(g):
        lhs, hs = lhs_s.at[g], hs_s.at[g]
        a, b = dot(tab[0], hs[0]), dot(tab[5], hs[1])
        for j, z in ((0, a + b), (1, a - b)):
            for m in range(2):
                for p in range(2):
                    for d in range(2):
                        at = (p, slice(m * n + j * h, m * n + (j + 1) * h), slice(d * h, (d + 1) * h))
                        lhs[at] = z[d * h : (d + 1) * h, (2 * m + p) * h : (2 * m + p + 1) * h].astype(BF16)

    def columns_back(g):
        lhs, far = lhs_s.at[g], far_s.at[g]
        a, b = dot(lhs[0], tab[2]), dot(lhs[1], tab[4])
        for j, z in ((0, a + b), (1, a - b)):
            far[j] = jnp.concatenate([z[:n], z[n:]], 1)

    def sums():
        for j in range(2):
            js = slice(j * h, (j + 1) * h)
            for m in range(2):
                s_re = s_im = None
                for g in range(group_size):
                    g_re, g_im = far_s[g, j, :, m * n : m * n + h], far_s[g, j, :, m * n + h : (m + 1) * n]
                    o_re, o_im = win_s[g, 0, :, js], win_s[g, 1, :, js]
                    a, b = o_re * g_re + o_im * g_im, o_re * g_im - o_im * g_re
                    s_re, s_im = (a, b) if s_re is None else (s_re + a, s_im + b)
                pg_ref[2 * m, :, :, js] += s_re.reshape(shards, rows, h)
                pg_ref[2 * m + 1, :, :, js] += s_im.reshape(shards, rows, h)
            s = None
            for g in range(group_size):
                o_re, o_im = win_s[g, 0, :, js], win_s[g, 1, :, js]
                v = o_re * o_re + o_im * o_im
                s = v if s is None else s + v
            pg_ref[4, :, :, js] += s.reshape(shards, rows, h)

    def scatter(g):
        base, fine, c = places[g]
        far = far_s.at[g]
        from_sub, from_lane = sub >= fine, lane >= c
        t = [[], []]
        for j in range(2):
            js = slice(j * h, (j + 1) * h)
            w = [None, None]
            for m in range(2):
                g_re, g_im = far[j, :, m * n : m * n + h], far[j, :, m * n + h : (m + 1) * n]
                p_re, p_im = probe_ref[m, 0, :, js], probe_ref[m, 1, :, js]
                v = (p_re * g_re + p_im * g_im, p_re * g_im - p_im * g_re)
                w = [x if y is None else x + y for x, y in zip(v, w)]
            for d in range(2):
                y = pltpu.roll(w[d].reshape(n // 8, 8, LANES), fine, 1)
                z = jnp.zeros((1, 8, LANES), F32)
                y = jnp.where(from_sub, jnp.concatenate([y, z], 0), jnp.concatenate([z, y], 0))
                t[d].append(pltpu.roll(y, c, 2))
        for d in range(2):
            a, b = t[d]
            out = [jnp.where(from_lane, a, 0.0), jnp.where(from_lane, b, a), jnp.where(from_lane, 0.0, b)]
            for q in range(3):
                grad[d, pl.ds(base + below_row, n + 8), LANES * q : LANES * (q + 1)] += out[q].reshape(n + 8, LANES)

    for stage in (load, wave, columns, down, weigh, up, columns_back):
        for g in range(group_size):
            stage(g)
    sums()
    for g in range(group_size):
        scatter(g)

    @pl.when(k == pl.num_programs(0) - 1)
    def _():
        if first:
            out = [(grad, grad_out), (pg_ref, pg_out), (loss_ref, loss_out)]
            out = [pltpu.make_async_copy(a, b, sems.at[i]) for i, (a, b) in enumerate(out)]
            for copy in out:
                copy.start()
            for copy in out:
                copy.wait()
            return
        out = [(grad.at[:, pl.ds(2 * n, n)], low_out), (grad.at[:, pl.ds(0, 2 * n)], grad_out), (away_ref, away_out), (keep_ref, keep_out)]
        out = [pltpu.make_async_copy(a, b, sems.at[i]) for i, (a, b) in enumerate(out)]
        out[0].start()
        out[1].start()
        me = off_ref[off_ref.shape[0] - 1, 0]
        loss = loss_ref[:, : n // 2] + loss_ref[:, n // 2 :]
        for core in (1, 0):
            ref = away_ref if core else keep_ref
            for slot in range(shards // 2):
                owner = owner_of(me, core, slot, shards)
                for q in range(5):
                    value = pg_ref[q, owner]
                    ref[slot, 2 * q * rows : (2 * q + 1) * rows] = value[:, : n // 2]
                    ref[slot, (2 * q + 1) * rows : (2 * q + 2) * rows] = value[:, n // 2 :]
                ref[slot, 10 * rows :] = loss
            out[3 - core].start()
        for copy in out:
            copy.wait()


def owner_of(me, core, slot, size):
    z = lax.rem(me // 4 + slot % (size // 4), size // 4)
    return z * 4 + ((me & 3) ^ (core + 2 * (slot // (size // 4))))


def windows(first, shards, count, offs, object_field, probe, amplitude, amp_first, table, carried=()):
    n = probe.shape[-1]
    width = object_field.shape[2]
    group_size = GROUP if first else count
    sums = (5, shards, n // shards, n)
    hbm, anywhere = pl.BlockSpec(memory_space=pltpu.HBM), pl.BlockSpec(memory_space=pl.ANY)
    inputs = (object_field, probe, amplitude, table, *carried)
    scratch = []
    if first:
        shapes = [(2, 2 * n, width), sums, (8, n)]
    else:
        slots = (shards // 2, 10 * (n // shards) + 8, n // 2)
        shapes = [(2, 2 * n, width), (2, n, width), slots, slots]
        scratch += [pltpu.VMEM(slots, F32)] * 2
    scratch += [
        pltpu.VMEM((2, 2 * n, width), F32),
        pltpu.VMEM((2, 2 * n if first else 3 * n, width), F32),
        pltpu.VMEM(sums, F32),
        pltpu.VMEM((8, n), F32),
        pltpu.VMEM(probe.shape, F32),
        pltpu.VMEM(table.shape, BF16),
        pltpu.VMEM((count // group_size, 2, group_size, n, LANES), F32),
        pltpu.VMEM((group_size, 2, n, n), F32),
        pltpu.VMEM((group_size, 2, 2 * n, n), BF16),
        pltpu.VMEM((group_size, 2, n, 2 * n), BF16),
        pltpu.VMEM((group_size, 2, n, 2 * n), F32),
        pltpu.SemaphoreType.DMA((12,)),
    ]
    return pl.pallas_call(
        functools.partial(windows_kernel, first, amp_first, group_size),
        grid_spec=pltpu.PrefetchScalarGridSpec(
            num_scalar_prefetch=1,
            grid=(count // group_size,),
            in_specs=[anywhere] * len(inputs),
            out_specs=[anywhere] * len(shapes),
            scratch_shapes=scratch,
        ),
        out_shape=[jax.ShapeDtypeStruct(s, F32) for s in shapes],
        compiler_params=pltpu.CompilerParams(vmem_limit_bytes=(48 if first else 27) << 20),
        name="near" if first else "across",
    )(offs, *inputs)


def place_kernel(nears, scale, me_ref, *refs):
    pieces, refs = refs[: len(nears)], refs[len(nears) :]
    if scale:
        losses_ref, out_ref, loss_ref, stage, sem = refs
    else:
        unused, out_ref, stage, sem = refs
    quarter, planes, rows, n = pieces[0].shape
    me = me_ref[0]
    copies = [pltpu.make_async_copy(piece, stage.at[i], sem.at[i, quarter]) for i, piece in enumerate(pieces)]
    for copy in copies:
        copy.start()
    if scale:
        loss = jnp.zeros(losses_ref.shape[1:], F32)
        for z in range(quarter):
            loss = loss + losses_ref[lax.rem(me // 4 + quarter - z, quarter)]
        loss_ref[0] = jnp.sum(loss) * scale
    out = []
    for i, near in enumerate(nears):
        copies[i].wait()
        for z in range(quarter):
            owner = owner_of(me, near, z, 4 * quarter)
            out.append(pltpu.make_async_copy(stage.at[i, z], out_ref.at[:, owner], sem.at[i, z]))
            out[-1].start()
    for copy in out:
        copy.wait()


def place(me, nears, pieces, losses=None, scale=None, base=None):
    quarter, planes, rows, n = pieces[0].shape
    shape = (planes, 4 * quarter, rows, n)
    anywhere, hbm = pl.BlockSpec(memory_space=pl.ANY), pl.BlockSpec(memory_space=pltpu.HBM)
    smem = pl.BlockSpec(memory_space=pltpu.SMEM)
    in_specs = [smem] + [anywhere] * len(pieces)
    out_specs, out_shape, aliases = [hbm], [jax.ShapeDtypeStruct(shape, F32)], {}
    if scale:
        in_specs, last = in_specs + [pl.BlockSpec(memory_space=pltpu.VMEM)], losses
        out_specs, out_shape = out_specs + [smem], out_shape + [jax.ShapeDtypeStruct((1,), F32)]
    else:
        in_specs, last = in_specs + [hbm], base
        aliases = {1 + len(pieces): 0}
    return pl.pallas_call(
        functools.partial(place_kernel, nears, scale),
        in_specs=in_specs,
        out_specs=out_specs,
        out_shape=out_shape,
        scratch_shapes=[
            pltpu.VMEM((len(nears), *pieces[0].shape), F32),
            pltpu.SemaphoreType.DMA((len(nears), quarter + 1)),
        ],
        input_output_aliases=aliases,
        compiler_params=pltpu.CompilerParams(vmem_limit_bytes=4 << 20),
        name="place",
    )(me.reshape(1), *pieces, last)


def swap(x, bit):
    size = lax.axis_size("row")
    return lax.ppermute(x, "row", [(i, i ^ bit) for i in range(size)])


def shift(x, by):
    size = lax.axis_size("row")
    return lax.ppermute(x, "row", [(i, (i + by) % size) for i in range(size)])


def tree(parts):
    while len(parts) > 1:
        parts = [sum(parts[i + 1 : i + 2], parts[i]) for i in range(0, len(parts), 2)]
    return parts[0]


def per_device(object_field, probe, amplitude, offsets):
    tile = object_field.shape[1]
    n = probe.shape[2]
    count = offsets.shape[0]
    near = count // 2
    size = lax.axis_size("row")
    me = lax.axis_index("row")
    table = jnp.asarray(dft_tables(n))
    below = lax.ppermute(object_field[:, :n], "row", [(i, i - 1) for i in range(1, size)])
    offs = jnp.concatenate([offsets - jnp.stack([me * tile, 0]), jnp.stack([me, 0])[None]])
    grad, pg, loss = windows(True, size, near, offs, object_field, probe, amplitude, 0, table)
    grad, low, keep, away = windows(
        False, size, count - near, offs, object_field, probe, amplitude, near, table, (below, grad, pg, loss)
    )
    hop = lax.ppermute(low, "row", [(i, i + 4) for i in range(3, size - 4, 4)])
    rows = n // size
    quarter = size // 4
    away = swap(away, 1)
    beside = swap(keep[quarter + 1 :] + away[quarter + 1 :], 2)
    x = keep[1:quarter] + away[1:quarter] + beside
    hop, x = lax.optimization_barrier((hop, x))
    own = keep[0] + away[0] + swap(keep[quarter] + away[quarter], 2)
    carried = jnp.where(me % 4 == 3, hop, low)
    carried = lax.ppermute(carried, "row", [(i, i - 3 if i % 4 == 3 else i + 1) for i in range(size)])
    parts = [own] + [shift(x[z - 1], 4 * z) for z in range(1, quarter)]
    total = tree(parts)
    losses = jnp.stack([p[10 * rows :] for p in parts])
    planes = total[: 10 * rows].reshape(5, 2, rows, n // 2)
    y = planes[:4] / jnp.sqrt(planes[4] + 1.0)
    y = jnp.concatenate([y[:, 0], y[:, 1]], -1)
    others = jnp.stack([shift(y, -4 * z) for z in range(1, quarter)])
    first = swap(y, 2)
    y = jnp.concatenate([y[None], others])
    sibling = swap(y, 1)
    beside = jnp.concatenate([first[None], swap(others, 2)])
    probe_dir, loss = place(me, (0,), (y,), losses, 1.0 / (count * size * n * n))
    object_grad = grad.at[:, :n].add(carried)
    probe_dir, object_grad, beside = lax.optimization_barrier((probe_dir, object_grad, beside))
    farther = swap(beside, 1)
    (probe_dir,) = place(me, (1, 2), (sibling, beside), base=probe_dir)
    (probe_dir,) = place(me, (3,), (farther,), base=probe_dir)
    probe_dir = probe_dir.reshape(2, 2, n, n)
    return (object_grad, probe_dir, loss)


def solution(mesh):
    placed = (
        P(None, ("groups", "row"), None),
        P(),
        P(("groups", "row"), None, None),
        P(("groups", "row"), None),
    )
    return jax.shard_map(
        per_device,
        mesh=mesh,
        in_specs=placed,
        out_specs=(P(None, ("groups", "row"), None), P("groups", None, None, None), P("groups")),
        check_vma=False,
    )
```

```python
import functools
import math

import jax
import jax.numpy as jnp
import ml_dtypes
import numpy as np
from jax import lax
from jax.experimental import pallas as pl
from jax.experimental.pallas import tpu as pltpu
from jax.sharding import PartitionSpec as P

F32, BF16 = jnp.float32, jnp.bfloat16
LANES = 128
VMEM_MIB = 30


def dft_tables(n):
    h = n // 2
    idx = np.arange(n)
    angle = (idx[:, None] * idx[None, :] % n).astype(np.float32) * np.float32(2.0 * math.pi / n)
    scale = np.float32(1.0 / math.sqrt(n))
    c, s = np.cos(angle) * scale, np.sin(angle) * scale
    near = np.arange(h)
    even, odd = 2 * near, 2 * near + 1
    turned = 2 * ((near + h // 2) % h) + 1

    def column(k):
        a, b = c[np.ix_(near, k)], s[np.ix_(near, k)]
        return np.block([[a, -b], [b, a]])

    def row(r):
        a, b = c[np.ix_(r, near)], s[np.ix_(r, near)]
        return np.block([[a, b], [-b, a]])

    tables = [column(even), column(turned), row(even), row(odd)]
    return np.stack(tables + [tables[1].T, tables[3].T]).astype(ml_dtypes.bfloat16)


def windows_kernel(first, amp_first, group_size, off_ref, *refs):
    object_ref, probe_hbm, amp_hbm, tab_hbm = refs[:4]
    if first:
        grad_out, pg_out, loss_out = refs[4:7]
    else:
        below_ref, grad_in, pg_in, loss_in, grad_out, low_out, keep_out, away_out, keep_ref, away_ref = refs[4:14]
    ext, grad, pg_ref, loss_ref, probe_ref, tab, amp_s, win_s, lhs_s, hs_s, far_s, sems = refs[-12:]
    shards, rows = pg_ref.shape[1:3]
    k = pl.program_id(0)
    n = probe_ref.shape[-1]
    h = n // 2
    width = ext.shape[2]
    below_row = 0 if first else n
    lane = lax.broadcasted_iota(jnp.int32, (1, 1, LANES), 2)
    sub = lax.broadcasted_iota(jnp.int32, (1, 8, 1), 1)

    def amplitude_copies(group):
        at = amp_first + group * group_size
        return [
            pltpu.make_async_copy(
                amp_hbm.at[pl.ds(at, group_size), :, pl.ds(q * LANES, LANES)], amp_s.at[group, q], sems.at[8 + 2 * group + q]
            )
            for q in range(2)
        ]

    if first:
        windows_in = [(object_ref, ext)]
        sums_in = []
    else:
        windows_in = [(object_ref.at[:, pl.ds(n, n)], ext.at[:, pl.ds(0, n)]), (below_ref, ext.at[:, pl.ds(n, n)])]
        sums_in = [(grad_in, grad.at[:, pl.ds(0, 2 * n)]), (pg_in, pg_ref), (loss_in, loss_ref)]
    windows_in = [*windows_in, (probe_hbm, probe_ref)]
    windows_in = [pltpu.make_async_copy(a, b, sems.at[i]) for i, (a, b) in enumerate(windows_in)]
    table_in = pltpu.make_async_copy(tab_hbm, tab, sems.at[3])
    sums_in = [pltpu.make_async_copy(a, b, sems.at[4 + i]) for i, (a, b) in enumerate(sums_in)]

    @pl.when(k == 0)
    def _():
        for copy in (*windows_in, table_in, *[c for i in range(amp_s.shape[0]) for c in amplitude_copies(i)], *sums_in):
            copy.start()
        if first:
            grad[...] = jnp.zeros_like(grad)
            pg_ref[...] = jnp.zeros_like(pg_ref)
            loss_ref[...] = jnp.zeros_like(loss_ref)
        else:
            grad[:, 2 * n :] = jnp.zeros((2, n, width), F32)
        for copy in (*windows_in, table_in, *sums_in):
            copy.wait()

    for copy in amplitude_copies(k):
        copy.wait()

    def dot(a, b):
        return jnp.dot(a, b, preferred_element_type=F32)

    places = []
    for g in range(group_size):
        r, c = off_ref[amp_first + k * group_size + g, 0] - below_row, off_ref[amp_first + k * group_size + g, 1]
        fine = lax.rem(r, 8)
        places.append((pl.multiple_of(r - fine, 8), fine, c))

    def load(g):
        base, fine, c = places[g]
        win = win_s.at[g]
        in_lane, in_sub = lane < LANES - c, sub < 8 - fine
        back_lane, back_sub = lax.rem(LANES - c, LANES), lax.rem(8 - fine, 8)
        for d in range(2):
            x = ext[d, pl.ds(base, n + 8), :].reshape(n // 8 + 1, 8, width)
            t = [pltpu.roll(x[:, :, LANES * q : LANES * (q + 1)], back_lane, 2) for q in range(3)]
            for q in range(2):
                y = pltpu.roll(jnp.where(in_lane, t[q], t[q + 1]), back_sub, 1)
                win[d, :, LANES * q : LANES * (q + 1)] = jnp.where(in_sub, y[:-1], y[1:]).reshape(n, LANES)

    def wave(g):
        win, lhs = win_s.at[g], lhs_s.at[g]
        for m in range(2):
            parts = []
            for j in range(2):
                js = slice(j * h, (j + 1) * h)
                p_re, p_im = probe_ref[m, 0, :, js], probe_ref[m, 1, :, js]
                o_re, o_im = win[0, :, js], win[1, :, js]
                parts.append((p_re * o_re - p_im * o_im, p_re * o_im + p_im * o_re))
            for d in range(2):
                at = (slice(m * n, (m + 1) * n), slice(d * h, (d + 1) * h))
                lhs[(0, *at)] = (parts[0][d] + parts[1][d]).astype(BF16)
                lhs[(1, *at)] = (parts[0][d] - parts[1][d]).astype(BF16)

    def columns(g):
        lhs, hs = lhs_s.at[g], hs_s.at[g]
        for p in range(2):
            v = dot(lhs[p], tab[p])
            for m in range(2):
                top, bottom = v[m * n : m * n + h], v[m * n + h : (m + 1) * n]
                for u, z in ((0, top + bottom), (1, top - bottom)):
                    for d in range(2):
                        at = (u, slice(d * h, (d + 1) * h), slice((2 * m + p) * h, (2 * m + p + 1) * h))
                        hs[at] = z[:, d * h : (d + 1) * h].astype(BF16)

    def down(g):
        hs, far = hs_s.at[g], far_s.at[g]
        for u in range(2):
            far[u] = dot(tab[2 + u], hs[u])

    idx = lax.broadcasted_iota(jnp.int32, (h, LANES), 1)
    lower = idx < LANES // 2
    pick_lo = jnp.where(lower, 2 * idx, 2 * idx - (LANES - 1))
    pick_hi = jnp.where(lower, 2 * idx + 1, 2 * idx - LANES)

    def weigh(g):
        hs, far = hs_s.at[g], far_s.at[g]
        total = jnp.zeros((8, n), F32)
        for u in range(2):
            lo = jnp.take_along_axis(amp_s[k, 0, g, pl.ds(u, h, stride=2), :], pick_lo, 1)
            hi = jnp.take_along_axis(amp_s[k, 1, g, pl.ds(u, h, stride=2), :], pick_hi, 1)
            amplitude = jnp.concatenate([jnp.where(lower, lo, hi), jnp.where(lower, hi, lo)], 1)
            power = None
            for e in range(2):
                for m in range(2):
                    f = far[u, e * h : (e + 1) * h, m * n : (m + 1) * n]
                    power = f * f if power is None else power + f * f
            magnitude = jnp.sqrt(power)
            miss = magnitude - amplitude
            total = total + jnp.sum((miss * miss).reshape(h // 8, 8, n), 0)
            weight = 0.25 * (1.0 - amplitude / jnp.maximum(magnitude, 0.5))
            for e in range(2):
                for m in range(2):
                    at = (u, slice(e * h, (e + 1) * h), slice(m * n, (m + 1) * n))
                    hs[at] = (weight * far[at]).astype(BF16)
        loss_ref[...] += total

    def up(g):
        lhs, hs = lhs_s.at[g], hs_s.at[g]
        a, b = dot(tab[0], hs[0]), dot(tab[5], hs[1])
        for j, z in ((0, a + b), (1, a - b)):
            for m in range(2):
                for p in range(2):
                    for d in range(2):
                        at = (p, slice(m * n + j * h, m * n + (j + 1) * h), slice(d * h, (d + 1) * h))
                        lhs[at] = z[d * h : (d + 1) * h, (2 * m + p) * h : (2 * m + p + 1) * h].astype(BF16)

    def columns_back(g):
        lhs, far = lhs_s.at[g], far_s.at[g]
        a, b = dot(lhs[0], tab[2]), dot(lhs[1], tab[4])
        for j, z in ((0, a + b), (1, a - b)):
            far[j] = jnp.concatenate([z[:n], z[n:]], 1)

    def sums():
        for j in range(2):
            js = slice(j * h, (j + 1) * h)
            for m in range(2):
                s_re = s_im = None
                for g in range(group_size):
                    g_re, g_im = far_s[g, j, :, m * n : m * n + h], far_s[g, j, :, m * n + h : (m + 1) * n]
                    o_re, o_im = win_s[g, 0, :, js], win_s[g, 1, :, js]
                    a, b = o_re * g_re + o_im * g_im, o_re * g_im - o_im * g_re
                    s_re, s_im = (a, b) if s_re is None else (s_re + a, s_im + b)
                pg_ref[2 * m, :, :, js] += s_re.reshape(shards, rows, h)
                pg_ref[2 * m + 1, :, :, js] += s_im.reshape(shards, rows, h)
            s = None
            for g in range(group_size):
                o_re, o_im = win_s[g, 0, :, js], win_s[g, 1, :, js]
                v = o_re * o_re + o_im * o_im
                s = v if s is None else s + v
            pg_ref[4, :, :, js] += s.reshape(shards, rows, h)

    def scatter(g):
        base, fine, c = places[g]
        far = far_s.at[g]
        from_sub, from_lane = sub >= fine, lane >= c
        t = [[], []]
        for j in range(2):
            js = slice(j * h, (j + 1) * h)
            w = [None, None]
            for m in range(2):
                g_re, g_im = far[j, :, m * n : m * n + h], far[j, :, m * n + h : (m + 1) * n]
                p_re, p_im = probe_ref[m, 0, :, js], probe_ref[m, 1, :, js]
                v = (p_re * g_re + p_im * g_im, p_re * g_im - p_im * g_re)
                w = [x if y is None else x + y for x, y in zip(v, w)]
            for d in range(2):
                y = pltpu.roll(w[d].reshape(n // 8, 8, LANES), fine, 1)
                z = jnp.zeros((1, 8, LANES), F32)
                y = jnp.where(from_sub, jnp.concatenate([y, z], 0), jnp.concatenate([z, y], 0))
                t[d].append(pltpu.roll(y, c, 2))
        for d in range(2):
            a, b = t[d]
            out = [jnp.where(from_lane, a, 0.0), jnp.where(from_lane, b, a), jnp.where(from_lane, 0.0, b)]
            for q in range(3):
                grad[d, pl.ds(base + below_row, n + 8), LANES * q : LANES * (q + 1)] += out[q].reshape(n + 8, LANES)

    for stage in (load, wave, columns, down, weigh, up, columns_back):
        for g in range(group_size):
            stage(g)
    sums()
    for g in range(group_size):
        scatter(g)

    @pl.when(k == pl.num_programs(0) - 1)
    def _():
        if first:
            out = [(grad, grad_out), (pg_ref, pg_out), (loss_ref, loss_out)]
            out = [pltpu.make_async_copy(a, b, sems.at[i]) for i, (a, b) in enumerate(out)]
            for copy in out:
                copy.start()
            for copy in out:
                copy.wait()
            return
        out = [(grad.at[:, pl.ds(2 * n, n)], low_out), (grad.at[:, pl.ds(0, 2 * n)], grad_out), (away_ref, away_out), (keep_ref, keep_out)]
        out = [pltpu.make_async_copy(a, b, sems.at[i]) for i, (a, b) in enumerate(out)]
        out[0].start()
        out[1].start()
        me = off_ref[off_ref.shape[0] - 1, 0]
        loss = loss_ref[:, : n // 2] + loss_ref[:, n // 2 :]
        for core in (1, 0):
            ref = away_ref if core else keep_ref
            for slot in range(shards // 2):
                owner = owner_of(me, core, slot, shards)
                for q in range(5):
                    value = pg_ref[q, owner]
                    ref[slot, 2 * q * rows : (2 * q + 1) * rows] = value[:, : n // 2]
                    ref[slot, (2 * q + 1) * rows : (2 * q + 2) * rows] = value[:, n // 2 :]
                ref[slot, 10 * rows :] = loss
            out[3 - core].start()
        for copy in out:
            copy.wait()


def owner_of(me, core, slot, size):
    z = lax.rem(me // 4 + slot % (size // 4), size // 4)
    return z * 4 + ((me & 3) ^ (core + 2 * (slot // (size // 4))))


def windows(first, shards, count, offs, object_field, probe, amplitude, amp_first, table, carried=()):
    n = probe.shape[-1]
    width = object_field.shape[2]
    group_size = count
    sums = (5, shards, n // shards, n)
    hbm, anywhere = pl.BlockSpec(memory_space=pltpu.HBM), pl.BlockSpec(memory_space=pl.ANY)
    inputs = (object_field, probe, amplitude, table, *carried)
    scratch = []
    if first:
        shapes = [(2, 2 * n, width), sums, (8, n)]
    else:
        slots = (shards // 2, 10 * (n // shards) + 8, n // 2)
        shapes = [(2, 2 * n, width), (2, n, width), slots, slots]
        scratch += [pltpu.VMEM(slots, F32)] * 2
    scratch += [
        pltpu.VMEM((2, 2 * n, width), F32),
        pltpu.VMEM((2, 2 * n if first else 3 * n, width), F32),
        pltpu.VMEM(sums, F32),
        pltpu.VMEM((8, n), F32),
        pltpu.VMEM(probe.shape, F32),
        pltpu.VMEM(table.shape, BF16),
        pltpu.VMEM((count // group_size, 2, group_size, n, LANES), F32),
        pltpu.VMEM((group_size, 2, n, n), F32),
        pltpu.VMEM((group_size, 2, 2 * n, n), BF16),
        pltpu.VMEM((group_size, 2, n, 2 * n), BF16),
        pltpu.VMEM((group_size, 2, n, 2 * n), F32),
        pltpu.SemaphoreType.DMA((12,)),
    ]
    return pl.pallas_call(
        functools.partial(windows_kernel, first, amp_first, group_size),
        grid_spec=pltpu.PrefetchScalarGridSpec(
            num_scalar_prefetch=1,
            grid=(count // group_size,),
            in_specs=[anywhere] * len(inputs),
            out_specs=[anywhere] * len(shapes),
            scratch_shapes=scratch,
        ),
        out_shape=[jax.ShapeDtypeStruct(s, F32) for s in shapes],
        compiler_params=pltpu.CompilerParams(vmem_limit_bytes=(48 if first else 27) << 20),
        name="near" if first else "across",
    )(offs, *inputs)


def place_kernel(nears, scale, me_ref, *refs):
    pieces, refs = refs[: len(nears)], refs[len(nears) :]
    if scale:
        losses_ref, out_ref, loss_ref, stage, sem = refs
    else:
        unused, out_ref, stage, sem = refs
    quarter, planes, rows, n = pieces[0].shape
    me = me_ref[0]
    copies = [pltpu.make_async_copy(piece, stage.at[i], sem.at[i, quarter]) for i, piece in enumerate(pieces)]
    for copy in copies:
        copy.start()
    if scale:
        loss = jnp.zeros(losses_ref.shape[1:], F32)
        for z in range(quarter):
            loss = loss + losses_ref[lax.rem(me // 4 + quarter - z, quarter)]
        loss_ref[0] = jnp.sum(loss) * scale
    out = []
    for i, near in enumerate(nears):
        copies[i].wait()
        for z in range(quarter):
            owner = owner_of(me, near, z, 4 * quarter)
            out.append(pltpu.make_async_copy(stage.at[i, z], out_ref.at[:, owner], sem.at[i, z]))
            out[-1].start()
    for copy in out:
        copy.wait()


def place(me, nears, pieces, losses=None, scale=None, base=None):
    quarter, planes, rows, n = pieces[0].shape
    shape = (planes, 4 * quarter, rows, n)
    anywhere, hbm = pl.BlockSpec(memory_space=pl.ANY), pl.BlockSpec(memory_space=pltpu.HBM)
    smem = pl.BlockSpec(memory_space=pltpu.SMEM)
    in_specs = [smem] + [anywhere] * len(pieces)
    out_specs, out_shape, aliases = [hbm], [jax.ShapeDtypeStruct(shape, F32)], {}
    if scale:
        in_specs, last = in_specs + [pl.BlockSpec(memory_space=pltpu.VMEM)], losses
        out_specs, out_shape = out_specs + [smem], out_shape + [jax.ShapeDtypeStruct((1,), F32)]
    else:
        in_specs, last = in_specs + [hbm], base
        aliases = {1 + len(pieces): 0}
    return pl.pallas_call(
        functools.partial(place_kernel, nears, scale),
        in_specs=in_specs,
        out_specs=out_specs,
        out_shape=out_shape,
        scratch_shapes=[
            pltpu.VMEM((len(nears), *pieces[0].shape), F32),
            pltpu.SemaphoreType.DMA((len(nears), quarter + 1)),
        ],
        input_output_aliases=aliases,
        compiler_params=pltpu.CompilerParams(vmem_limit_bytes=4 << 20),
        name="place",
    )(me.reshape(1), *pieces, last)


def swap(x, bit):
    size = lax.axis_size("row")
    return lax.ppermute(x, "row", [(i, i ^ bit) for i in range(size)])


def shift(x, by):
    size = lax.axis_size("row")
    return lax.ppermute(x, "row", [(i, (i + by) % size) for i in range(size)])


def tree(parts):
    while len(parts) > 1:
        parts = [sum(parts[i + 1 : i + 2], parts[i]) for i in range(0, len(parts), 2)]
    return parts[0]


def per_device(object_field, probe, amplitude, offsets):
    tile = object_field.shape[1]
    n = probe.shape[2]
    count = offsets.shape[0]
    near = count // 2
    size = lax.axis_size("row")
    me = lax.axis_index("row")
    table = jnp.asarray(dft_tables(n))
    below = lax.ppermute(object_field[:, :n], "row", [(i, i - 1) for i in range(1, size)])
    offs = jnp.concatenate([offsets - jnp.stack([me * tile, 0]), jnp.stack([me, 0])[None]])
    grad, pg, loss = windows(True, size, near, offs, object_field, probe, amplitude, 0, table)
    grad, low, keep, away = windows(
        False, size, count - near, offs, object_field, probe, amplitude, near, table, (below, grad, pg, loss)
    )
    hop = lax.ppermute(low, "row", [(i, i + 4) for i in range(3, size - 4, 4)])
    rows = n // size
    quarter = size // 4
    away = swap(away, 1)
    beside = swap(keep[quarter + 1 :] + away[quarter + 1 :], 2)
    x = keep[1:quarter] + away[1:quarter] + beside
    hop, x = lax.optimization_barrier((hop, x))
    own = keep[0] + away[0] + swap(keep[quarter] + away[quarter], 2)
    carried = jnp.where(me % 4 == 3, hop, low)
    carried = lax.ppermute(carried, "row", [(i, i - 3 if i % 4 == 3 else i + 1) for i in range(size)])
    parts = [own] + [shift(x[z - 1], 4 * z) for z in range(1, quarter)]
    total = tree(parts)
    losses = jnp.stack([p[10 * rows :] for p in parts])
    planes = total[: 10 * rows].reshape(5, 2, rows, n // 2)
    y = planes[:4] / jnp.sqrt(planes[4] + 1.0)
    y = jnp.concatenate([y[:, 0], y[:, 1]], -1)
    others = jnp.stack([shift(y, -4 * z) for z in range(1, quarter)])
    first = swap(y, 2)
    y = jnp.concatenate([y[None], others])
    sibling = swap(y, 1)
    beside = jnp.concatenate([first[None], swap(others, 2)])
    probe_dir, loss = place(me, (0,), (y,), losses, 1.0 / (count * size * n * n))
    object_grad = grad.at[:, :n].add(carried)
    probe_dir, object_grad, beside = lax.optimization_barrier((probe_dir, object_grad, beside))
    farther = swap(beside, 1)
    (probe_dir,) = place(me, (1, 2), (sibling, beside), base=probe_dir)
    (probe_dir,) = place(me, (3,), (farther,), base=probe_dir)
    probe_dir = probe_dir.reshape(2, 2, n, n)
    return (object_grad, probe_dir, loss)


def solution(mesh):
    placed = (
        P(None, ("groups", "row"), None),
        P(),
        P(("groups", "row"), None, None),
        P(("groups", "row"), None),
    )
    return jax.shard_map(
        per_device,
        mesh=mesh,
        in_specs=placed,
        out_specs=(P(None, ("groups", "row"), None), P("groups", None, None, None), P("groups")),
        check_vma=False,
    )
```
